32 devices in a mesh: lat: 8 (over z, x), fld: 4 (over y, core).
Axes of the slice: x: 2, y: 2, z: 4, core: 2. Of those that a mesh axis runs over, the one named last changes fastest.
Arguments:
- field_grid: bfloat16 [8, 2560, 5120], P('fld', 'lat'), may hold values from -300 to 300
- wave_table: int32 [64], replicated, may hold values from 0 to 1279, as said below
- legendre: bfloat16 [64, 2, 640, 1280], P('lat', None, 'fld'), may hold values from -0.15625 to 0.15625
Outputs:
- spectral: float32 [64, 640, 32], P('lat', 'fld')
The draws below stay inside these ranges and needn't reach their ends.
Inputs may be any that keep to these rules, and one draw needn't show every extreme that they name: `wave_table`: the entries differ from one another; each aligned block of 8 entries owned by one index of lat is made of pairs m and 1279 - m, next to each other.
All inputs are finite; a program needn't handle non-finite values.
Results may differ from the reference program's by a relative error of at most 0.0048.
Values may be sent and summed in bfloat16 or wider, within the bound.
A program may use at most 64 MiB of HBM per device.

```python
import math
import jax
import jax.numpy as jnp
from jax import lax

NLAT = 2560
NLON = 5120
TRUNC = 1280
FIELDS = 8
SLOTS = 64


def draw_wave_table(key, part):
    pair_count = TRUNC // 2
    chosen = jax.random.permutation(jax.random.fold_in(key, 11), pair_count - 1)[:SLOTS // 2 - 1] + 1
    chosen = jnp.concatenate([jnp.zeros((1,), jnp.int32), chosen.astype(jnp.int32)])
    chosen = jax.random.permutation(jax.random.fold_in(key, 12), chosen)
    paired = jnp.stack([chosen, TRUNC - 1 - chosen], axis=1)
    return paired.reshape(SLOTS).astype(jnp.int32)


def block_scale(key, dims, pieces, least, top_value):
    loudness = 1.0
    for dim, shards_of in pieces:
        steps = jax.random.uniform(jax.random.fold_in(jax.random.fold_in(key, 6), dim), (shards_of,), jnp.float32, least / len(pieces), top_value / len(pieces))
        loudness = loudness * jnp.repeat(jnp.exp(steps), dims[dim] // shards_of).reshape((-1,) + (1,) * (len(dims) - 1 - dim))
    return loudness


def noise(stream_key, extent, spread, most, shards=(), kind=jnp.bfloat16):
    drawn = jax.random.normal(stream_key, extent, jnp.float32) * spread
    if len(shards) > 0:
        drawn = block_scale(stream_key, extent, shards, -0.22, 0.18) * drawn
    return jnp.clip(drawn, min=-most, max=most).astype(kind)


def setup_inputs(seed: int = 0) -> dict:
    keys = jax.random.split(jax.random.key(seed), 4)
    return {
        "field_grid": noise(keys[0], (FIELDS, NLAT, NLON), 50.0, 300.0, ((0, 4), (1, 8))),
        "wave_table": draw_wave_table(jax.random.fold_in(keys[3], 71), 0),
        "legendre": noise(keys[2], (SLOTS, 2, TRUNC // 2, NLAT // 2), (NLAT // 2) ** -0.5, 0.15625, ((0, 8), (2, 4))),
    }


TWO_PI = 2.0 * math.pi


def twiddle_block(wave_block, lon_total):
    lon_index = jnp.arange(lon_total, dtype=jnp.int32)
    phase_index = (wave_block[:, None].astype(jnp.int32) * lon_index[None, :]) % lon_total
    angles = phase_index.astype(jnp.float32) * (TWO_PI / lon_total)
    cosine_sine = jnp.stack([jnp.cos(angles), -jnp.sin(angles)], axis=1)
    return cosine_sine.reshape(2 * wave_block.shape[0], lon_total).astype(jnp.bfloat16)


def fold_halves(fourier):
    half_lat = fourier.shape[-1] // 2
    north_rows = fourier[..., :half_lat].astype(jnp.float32)
    south_rows = jnp.flip(fourier[..., half_lat:], axis=-1).astype(jnp.float32)
    return jnp.stack([north_rows + south_rows, north_rows - south_rows], axis=1).astype(jnp.bfloat16)


def reference(field_grid, wave_table, legendre):
    grid_rows = field_grid.reshape(FIELDS * NLAT, NLON).astype(jnp.float32)
    block_size = math.gcd(SLOTS, 256)
    wave_blocks = wave_table.reshape(SLOTS // block_size, block_size)

    def transform(wave_block):
        twiddle = twiddle_block(wave_block, NLON).astype(jnp.float32)
        spectra = lax.dot_general(twiddle, grid_rows, (((1,), (1,)), ((), ())), precision=lax.Precision.HIGHEST, preferred_element_type=jnp.float32)
        return (spectra * (1.0 / NLON)).astype(jnp.bfloat16)

    fourier = lax.map(transform, wave_blocks).reshape(SLOTS, 2, FIELDS, NLAT)
    folded = fold_halves(fourier).reshape(SLOTS, 2, 2 * FIELDS, NLAT // 2)
    row_index = jnp.arange(TRUNC // 2, dtype=jnp.int32)
    parity = jnp.arange(2, dtype=jnp.int32)

    def contract(inputs):
        table_slot, folded_slot, wave = inputs
        coeffs = jnp.einsum("prj,pcj->rpc", table_slot.astype(jnp.float32), folded_slot.astype(jnp.float32), precision=lax.Precision.HIGHEST)
        degree = wave + 2 * row_index[:, None] + parity[None, :]
        valid_mask = (degree <= TRUNC - 1).astype(jnp.float32)
        return (coeffs * valid_mask[:, :, None]).reshape(TRUNC // 2, 4 * FIELDS)

    return lax.map(contract, (legendre, folded, wave_table))
```

```python
import functools
import math

import jax
import jax.numpy as jnp
from jax import lax
from jax.experimental import pallas as pl
from jax.experimental.pallas import tpu as pltpu
from jax.sharding import PartitionSpec as P

TWO_PI = 2.0 * math.pi


def twiddle_block(wave_block, lon_total):
    fine_count = math.gcd(lon_total, 128)
    coarse_count = lon_total // fine_count
    waves = wave_block[:, None]
    coarse_index = (
        waves * (jnp.arange(coarse_count, dtype=jnp.int32) * fine_count)[None, :] % lon_total
    )
    fine_index = waves * jnp.arange(fine_count, dtype=jnp.int32)[None, :] % lon_total
    coarse_angle = coarse_index.astype(jnp.float32) * (TWO_PI / lon_total)
    fine_angle = fine_index.astype(jnp.float32) * (TWO_PI / lon_total)
    coarse_cos = jnp.cos(coarse_angle)[:, :, None]
    coarse_sin = jnp.sin(coarse_angle)[:, :, None]
    fine_cos = jnp.cos(fine_angle)[:, None, :]
    fine_sin = jnp.sin(fine_angle)[:, None, :]
    cosine = (coarse_cos * fine_cos - coarse_sin * fine_sin).reshape(wave_block.shape[0], lon_total)
    minus_sine = (-(coarse_sin * fine_cos + coarse_cos * fine_sin)).reshape(
        wave_block.shape[0], lon_total
    )
    return jnp.concatenate([cosine, minus_sine], axis=0).astype(jnp.bfloat16)


def fold_halves(fourier):
    half_lat = fourier.shape[-1] // 2
    north_rows = fourier[..., :half_lat].astype(jnp.float32)
    south_rows = jnp.flip(fourier[..., half_lat:], axis=-1).astype(jnp.float32)
    return jnp.stack([north_rows + south_rows, north_rows - south_rows], axis=1).astype(
        jnp.bfloat16
    )


def shards_by_collectives(field_grid, wave_table, legendre):
    f_dev, lat_dev, lon_total = field_grid.shape
    slot_total = wave_table.shape[0]
    slot_dev = legendre.shape[0]
    row_dev = legendre.shape[2]
    grid_rows = field_grid.reshape(f_dev * lat_dev, lon_total)
    block_size = math.gcd(slot_total, 256)
    wave_blocks = wave_table.reshape(slot_total // block_size, block_size)

    def transform(wave_block):
        twiddle = twiddle_block(wave_block, lon_total)
        spectra = lax.dot_general(
            twiddle, grid_rows, (((1,), (1,)), ((), ())), preferred_element_type=jnp.float32
        )
        spectra = (spectra * (1.0 / lon_total)).astype(jnp.bfloat16)
        return jnp.transpose(spectra.reshape(2, block_size, f_dev, lat_dev), (1, 0, 2, 3))

    fourier = lax.map(transform, wave_blocks).reshape(slot_total, 2, f_dev, lat_dev)
    first_slot = lax.axis_index("lat") * slot_dev
    own_waves = lax.dynamic_slice_in_dim(wave_table, first_slot, slot_dev)
    trunc_total = 2 * row_dev * lax.axis_size("fld")
    row_index = lax.axis_index("fld") * row_dev + jnp.arange(row_dev, dtype=jnp.int32)
    parity = jnp.arange(2, dtype=jnp.int32)
    degree = own_waves[:, None, None] + 2 * row_index[None, :, None] + parity[None, None, :]
    valid_mask = (degree <= trunc_total - 1).astype(jnp.float32)
    regrouped = lax.all_to_all(fourier, "lat", split_axis=0, concat_axis=3, tiled=True)
    folded = fold_halves(regrouped)
    folded_piece = lax.all_gather(folded, "fld", axis=3, tiled=True)
    parts_count = folded_piece.shape[2]
    width = folded_piece.shape[3]
    merged = folded_piece.reshape(slot_dev, 2, parts_count * width, folded_piece.shape[4])
    coeffs = jnp.einsum("sprj,spcj->srpc", legendre, merged, preferred_element_type=jnp.float32)
    coeffs = coeffs.reshape(slot_dev, row_dev, 2, parts_count, width)
    coeffs = coeffs * valid_mask[:, :, :, None, None]
    return coeffs.reshape(slot_dev, row_dev, -1)


LANES = 128
HALF = 64
MESH = pl.DeviceIdType.MESH


def sin_cos_of_phase(phase, period):
    turns = jnp.floor(phase * (1.0 / period))
    rest = phase - turns * period
    rest = jnp.where(rest < 0, rest + period, rest)
    rest = jnp.where(rest >= period, rest - period, rest)
    eighth = period / 8
    q0 = rest < eighth
    q1 = rest < 3 * eighth
    q2 = rest < 5 * eighth
    q3 = rest < 7 * eighth
    centre = jnp.where(
        q0, 0.0, jnp.where(q1, 2 * eighth, jnp.where(q2, 4 * eighth, jnp.where(q3, 6 * eighth, period)))
    )
    x = (rest - centre) * (TWO_PI / period)
    y = x * x
    s = x * (1.0 + y * (-1 / 6 + y * (1 / 120 + y * (-1 / 5040 + y * (1 / 362880)))))
    c = 1.0 + y * (-1 / 2 + y * (1 / 24 + y * (-1 / 720 + y * (1 / 40320 - y * (1 / 3628800)))))
    even = q0 | (q2 & ~q1) | ~q3
    minus_sin = (q3 & ~q1)
    minus_cos = (q2 & ~q0)
    sine = jnp.where(even, s, c)
    sine = jnp.where(minus_sin, -sine, sine)
    cosine = jnp.where(even, c, s)
    cosine = jnp.where(minus_cos, -cosine, cosine)
    return sine, cosine


def transform_kernel(
    lat_count, wave_hbm, wave_row_hbm, field_ref, legendre_ref, out_ref,
    grid, twiddle, coarse, table, send, recv, folded, partial, spun, wave_smem, wave_row,
    field_sem, wave_sem, table_sem, sent, lat_recv, y_recv, c_recv, d_recv,
):
    lat = lax.axis_index("lat")
    fld = lax.axis_index("fld")
    y_peer = (fld + 2) % 4
    partner = fld + 1 - 2 * (fld % 2)
    partner_y = (partner + 2) % 4

    _, lat_dev, lon_total = field_ref.shape
    main = lat_dev // LANES
    tiles = 2 * main + 1
    slot_dev, _, row_dev, _ = legendre_ref.shape
    slot_total = wave_row_hbm.shape[1]
    half_lats = lat_count // 2
    chunk_tiles = ((0, 1), (1, main + 1), (main + 1, tiles))
    chunk_count = len(chunk_tiles)

    def band_of(index):
        south = index // half_lats
        return south, index + south * (lat_count - 1 - 2 * index)

    def place_of(index):
        south, band = band_of(index)
        return 2 * band + south

    south, band = band_of(lat)
    place = place_of(lat)
    odd = band % 2
    mixed = (south + odd) % 2

    def chunk_of(t):
        return [low <= t < high for low, high in chunk_tiles].index(True)

    def load(f, row, count, dst):
        pltpu.make_async_copy(
            field_ref.at[f, pl.ds(pl.multiple_of(row, HALF), count)],
            grid.at[pl.ds(pl.multiple_of(dst, HALF), count)],
            field_sem.at[chunk_of(load_tile[0])],
        ).start(priority=1)

    load_tile = [0]

    def load_main(f, t, dst_tile):
        load_tile[0] = dst_tile
        north_row = LANES * t + HALF * odd
        south_row = lat_dev - LANES - LANES * t - HALF * odd
        load(f, north_row + south * (south_row - north_row), LANES, LANES * dst_tile)

    wave_copies = [
        pltpu.make_async_copy(wave_row_hbm, wave_row, wave_sem.at[0]),
        pltpu.make_async_copy(wave_hbm, wave_smem, wave_sem.at[1]),
    ]
    for copy in wave_copies:
        copy.start()
    for t in range(main):
        load_main(0, t, t)
    load_tile[0] = main
    tail_row = (lat_dev - HALF) * (1 - mixed)
    load(0, tail_row, HALF, LANES * main + HALF * mixed)
    load(1, tail_row, HALF, LANES * main + HALF * (1 - mixed))
    for t in range(main):
        load_main(1, t, main + 1 + t)

    barrier = pltpu.get_barrier_semaphore()
    for d in range(1, lat_count):
        pl.semaphore_signal(
            barrier, inc=1, device_id=((lat + d) % lat_count, fld), device_id_type=MESH
        )
    for other in (y_peer, partner):
        pl.semaphore_signal(barrier, inc=1, device_id=(lat, other), device_id_type=MESH)

    for copy in wave_copies:
        copy.wait()
    waves = wave_row[...].astype(jnp.float32)
    waves = jnp.concatenate([waves, waves], axis=1)
    width = 2 * slot_total
    coarse_count = lon_total // LANES
    k_fine = lax.broadcasted_iota(jnp.int32, (LANES, width), 0).astype(jnp.float32)
    is_sine = lax.broadcasted_iota(jnp.int32, (LANES, width), 1) >= slot_total
    quarter = jnp.where(is_sine, lon_total / 4, 0.0)
    fine_sin, fine_cos = sin_cos_of_phase(waves * k_fine + quarter, lon_total)
    coarse_rows = coarse.shape[1]
    k_coarse = lax.broadcasted_iota(jnp.int32, (coarse_rows, width), 0).astype(jnp.float32) * LANES
    coarse_sin, coarse_cos = sin_cos_of_phase(waves * k_coarse, lon_total)
    coarse[0] = coarse_sin
    coarse[1] = coarse_cos
    for a in range(coarse_count):
        block = coarse[1, pl.ds(a, 1), :] * fine_cos - coarse[0, pl.ds(a, 1), :] * fine_sin
        twiddle[pl.ds(a * LANES, LANES), :] = block.astype(jnp.bfloat16)

    row = lax.broadcasted_iota(jnp.int32, (LANES, LANES), 0)
    column = lax.broadcasted_iota(jnp.int32, (LANES, LANES), 1)
    turned = row + south * (LANES - 1 - 2 * row)
    order = (turned == column).astype(jnp.float32).astype(jnp.bfloat16)

    def flipped(d):
        index, bit = lat, 1
        while bit < lat_count:
            if d & bit:
                index = index + bit * (1 - 2 * ((lat // bit) % 2))
            bit *= 2
        return index

    def columns(q):
        low, high = chunk_tiles[q]
        return pl.ds(low * LANES, (high - low) * LANES)

    def remote(src, dst, sent_at, recv_at, device):
        return pltpu.make_async_remote_copy(
            src_ref=src, dst_ref=dst, send_sem=sent.at[sent_at], recv_sem=recv_at,
            device_id=device, device_id_type=MESH,
        )

    def y_group(d, q):
        if d < half_lats:
            return d
        return half_lats + 2 * (d - half_lats) + (q == chunk_count - 1)

    def pass_on(src, source_place, d, q):
        here = recv.at[fld, source_place, :, columns(q)]
        remote(src, here, 1, y_recv.at[y_group(d, q)], (lat, y_peer)).start()
        remote(src, here, 2, c_recv.at[source_place // half_lats], (lat, partner)).start()

    for q in range(chunk_count):
        low, high = chunk_tiles[q]
        rows = pl.ds(low * LANES, (high - low) * LANES)
        pltpu.make_async_copy(grid.at[rows], grid.at[rows], field_sem.at[q]).wait()
        spectra = jnp.dot(grid[rows, :], twiddle[...], preferred_element_type=jnp.float32)
        spectra = (spectra * (1.0 / lon_total)).astype(jnp.bfloat16)
        for t in range(low, high):
            part = spectra[(t - low) * LANES:(t - low + 1) * LANES, :]
            part = jnp.dot(order, part, preferred_element_type=jnp.float32)
            part = part.T
            for owner in range(lat_count):
                s0 = owner * slot_dev
                send[owner, :, pl.ds(t * LANES, LANES)] = jnp.concatenate(
                    [part[s0:s0 + slot_dev], part[slot_total + s0:slot_total + s0 + slot_dev]], axis=0
                ).astype(jnp.bfloat16)
        if q == 0:
            pl.semaphore_wait(barrier, lat_count + 1)
        for d in range(lat_count - 1, 0, -1):
            owner = flipped(d)
            remote(
                send.at[owner, :, columns(q)], recv.at[fld, place, :, columns(q)],
                0, lat_recv.at[d - 1, q], (owner, fld),
            ).start()
        pass_on(send.at[lat, :, columns(q)], place, 0, q)
        recv[fld, place, :, columns(q)] = send[lat, :, columns(q)]

    table_copy = pltpu.make_async_copy(legendre_ref, table, table_sem)
    table_copy.start()

    def hops(d):
        return (d & 1) + d // 2

    when = (2.2, 3.3, 4.4)
    events = []
    for d in range(lat_count):
        for q in range(chunk_count):
            arrival = when[q] + 1.45 * hops(d)
            if d:
                events.append((arrival, 0, d, q))
            if q == chunk_count - 1 or y_group(d, q) != y_group(d, q + 1):
                events.append((arrival + (1.9 if d else 2.4), 1, d, q))
    for _, kind, d, q in sorted(events):
        source = flipped(d)
        source_place = place_of(source)
        if kind == 0:
            here = recv.at[fld, source_place, :, columns(q)]
            remote(here, here, 0, lat_recv.at[d - 1, q], (lat, y_peer)).wait_recv()
            pass_on(here, source_place, d, q)
        else:
            members = [k for k in range(chunk_count) if y_group(d, k) == y_group(d, q)]
            low, high = chunk_tiles[members[0]][0], chunk_tiles[members[-1]][1]
            there = recv.at[y_peer, source_place, :, pl.ds(low * LANES, (high - low) * LANES)]
            remote(there, there, 1, y_recv.at[y_group(d, q)], (lat, y_peer)).wait_recv()
            remote(there, there, 3, d_recv.at[source_place // half_lats], (lat, partner)).start()

    depth = 2 * slot_dev
    pair_lats = 2 * lat_dev
    low_half = lax.broadcasted_iota(jnp.int32, (depth, LANES), 1) < HALF
    total_rows = 8 * depth
    trunc_total = 2 * row_dev * 4
    slot_of = lax.broadcasted_iota(jnp.int32, (row_dev, total_rows), 1) % slot_dev
    degree_row = 2 * (lax.broadcasted_iota(jnp.int32, (row_dev, total_rows), 0) + fld * row_dev)
    wave_of = jnp.zeros((1, total_rows), jnp.int32)
    for s in range(slot_dev):
        wave_of = jnp.where(slot_of[:1] == s, wave_smem[lat * slot_dev + s], wave_of)
    table_copy.wait()
    for h in range(half_lats // 2 - 1, -1, -1):
        for group, sem in ((partner, c_recv), (partner_y, d_recv)):
            block = recv.at[group, pl.ds(h * half_lats, half_lats)]
            remote(block, block, 3, sem.at[h], (lat, partner)).wait_recv()
        base = h * pair_lats
        for group in range(4):
            north = [recv[group, 2 * (2 * h + o)].astype(jnp.float32) for o in range(2)]
            mirror = [recv[group, 2 * (2 * h + o) + 1].astype(jnp.float32) for o in range(2)]
            for p in range(2):
                even_band, odd_band = [
                    n + m if p == 0 else n - m for n, m in zip(north, mirror)
                ]
                cut = main * LANES
                mid_even = even_band[:, cut:cut + LANES]
                mid_odd = odd_band[:, cut:cut + LANES]
                mid = (
                    jnp.where(low_half, mid_even, mid_odd),
                    pltpu.roll(jnp.where(low_half, mid_odd, mid_even), HALF, 1),
                )
                for f in range(2):
                    start = f * (cut + LANES)
                    rows = pl.ds((2 * group + f) * depth, depth)
                    folded[p, rows, pl.ds(base, cut)] = even_band[:, start:start + cut].astype(jnp.bfloat16)
                    folded[p, rows, pl.ds(base + cut, LANES)] = mid[f].astype(jnp.bfloat16)
                    folded[p, rows, pl.ds(base + cut + LANES, cut)] = odd_band[
                        :, start:start + cut
                    ].astype(jnp.bfloat16)
        for p in range(2):
            kept = jnp.zeros((row_dev, total_rows), jnp.float32)
            for s in range(slot_dev):
                sums = lax.dot_general(
                    table[s, p, :, pl.ds(base, pair_lats)], folded[p, :, pl.ds(base, pair_lats)],
                    (((1,), (1,)), ((), ())), preferred_element_type=jnp.float32,
                )
                kept = jnp.where(slot_of == s, sums, kept)
            if h > 0:
                partial[p] = kept
                continue
            kept = jnp.where(degree_row + (wave_of + p) <= trunc_total - 1, kept + partial[p], 0.0)
            padded = jnp.concatenate(
                [kept, jnp.zeros((spun.shape[1] * LANES - row_dev, total_rows), jnp.float32)], axis=0
            )
            for t in range(spun.shape[1]):
                spun[p, t] = padded[t * LANES:(t + 1) * LANES].T
    for s in range(slot_dev):
        for p in range(2):
            for c in range(2):
                for t in range(spun.shape[1]):
                    kept_rows = min(LANES, row_dev - t * LANES)
                    out_ref[s, pl.ds(p * 16 + c * 8, 8), pl.ds(t * LANES, kept_rows)] = spun[
                        p, t, pl.ds(c * slot_dev + s, 8, stride=depth), :
                    ][:, :kept_rows]
    for kind, count in ((0, lat_count - 1), (1, lat_count), (2, lat_count), (3, lat_count)):
        block = recv.at[fld, pl.ds(0, count)]
        remote(block, block, kind, table_sem, (lat, partner)).wait_send()


def shards_by_kernel(field_grid, wave_table, legendre):
    f_dev, lat_dev, lon_total = field_grid.shape
    slot_dev, _, row_dev, north_total = legendre.shape
    slot_total = wave_table.shape[0]
    lat_count = lax.axis_size("lat")
    rows = f_dev * lat_dev
    bf16, f32 = jnp.bfloat16, jnp.float32
    dma = pltpu.SemaphoreType.DMA
    padded_rows = -(-row_dev // LANES) * LANES
    coarse_rows = -(-(lon_total // LANES) // 8) * 8
    vmem, smem = pltpu.VMEM, pltpu.SMEM
    out = pl.pallas_call(
        functools.partial(transform_kernel, lat_count),
        out_shape=pltpu.VMEM((slot_dev, 32, row_dev), f32),
        in_specs=[pl.BlockSpec(memory_space=pl.ANY)] * 4,
        out_specs=pl.BlockSpec(memory_space=vmem),
        scratch_shapes=[
            vmem((rows, lon_total), bf16),
            vmem((lon_total, 2 * slot_total), bf16),
            vmem((2, coarse_rows, 2 * slot_total), f32),
            vmem(legendre.shape, bf16),
            vmem((lat_count, 2 * slot_dev, rows), bf16),
            vmem((4, lat_count, 2 * slot_dev, rows), bf16),
            vmem((2, 16 * slot_dev, north_total), bf16),
            vmem((2, row_dev, 16 * slot_dev), f32),
            vmem((2, padded_rows // LANES, 16 * slot_dev, LANES), f32),
            smem((slot_total,), jnp.int32),
            vmem((1, slot_total), jnp.int32),
            dma((3,)),
            dma((2,)),
            dma(()),
            dma((4,)),
            dma((lat_count - 1, 3)),
            dma((3 * lat_count // 2,)),
            dma((2,)),
            dma((2,)),
        ],
        compiler_params=pltpu.CompilerParams(
            collective_id=0, has_side_effects=True
        ),
    )(wave_table, wave_table.reshape(1, slot_total), field_grid, legendre)
    return jnp.transpose(out, (0, 2, 1))


def shards(field_grid, wave_table, legendre):
    f_dev, lat_dev, lon_total = field_grid.shape
    slot_dev, _, row_dev, _ = legendre.shape
    slot_total = wave_table.shape[0]
    fits = (
        f_dev == 2
        and slot_dev == 8
        and 2 * slot_total == LANES
        and lat_dev % LANES == HALF
        and lat_dev > LANES
        and lax.axis_size("fld") == 4
        and lax.axis_size("lat") == 8
        and lon_total % LANES == 0
        and row_dev % 8 == 0
        and 2 * row_dev * 4 * lon_total < 2**24
    )
    if fits:
        return shards_by_kernel(field_grid, wave_table, legendre)
    return shards_by_collectives(field_grid, wave_table, legendre)


def solution(mesh):
    placed = (P("fld", "lat", None), P(), P("lat", None, "fld", None))
    return jax.shard_map(
        shards, mesh=mesh, in_specs=placed, out_specs=P("lat", "fld", None), check_vma=False
    )
```

```python
import functools
import math

import jax
import jax.numpy as jnp
from jax import lax
from jax.experimental import pallas as pl
from jax.experimental.pallas import tpu as pltpu
from jax.sharding import PartitionSpec as P

TWO_PI = 2.0 * math.pi


def twiddle_block(wave_block, lon_total):
    fine_count = math.gcd(lon_total, 128)
    coarse_count = lon_total // fine_count
    waves = wave_block[:, None]
    coarse_index = (
        waves * (jnp.arange(coarse_count, dtype=jnp.int32) * fine_count)[None, :] % lon_total
    )
    fine_index = waves * jnp.arange(fine_count, dtype=jnp.int32)[None, :] % lon_total
    coarse_angle = coarse_index.astype(jnp.float32) * (TWO_PI / lon_total)
    fine_angle = fine_index.astype(jnp.float32) * (TWO_PI / lon_total)
    coarse_cos = jnp.cos(coarse_angle)[:, :, None]
    coarse_sin = jnp.sin(coarse_angle)[:, :, None]
    fine_cos = jnp.cos(fine_angle)[:, None, :]
    fine_sin = jnp.sin(fine_angle)[:, None, :]
    cosine = (coarse_cos * fine_cos - coarse_sin * fine_sin).reshape(wave_block.shape[0], lon_total)
    minus_sine = (-(coarse_sin * fine_cos + coarse_cos * fine_sin)).reshape(
        wave_block.shape[0], lon_total
    )
    return jnp.concatenate([cosine, minus_sine], axis=0).astype(jnp.bfloat16)


def fold_halves(fourier):
    half_lat = fourier.shape[-1] // 2
    north_rows = fourier[..., :half_lat].astype(jnp.float32)
    south_rows = jnp.flip(fourier[..., half_lat:], axis=-1).astype(jnp.float32)
    return jnp.stack([north_rows + south_rows, north_rows - south_rows], axis=1).astype(
        jnp.bfloat16
    )


def shards_by_collectives(field_grid, wave_table, legendre):
    f_dev, lat_dev, lon_total = field_grid.shape
    slot_total = wave_table.shape[0]
    slot_dev = legendre.shape[0]
    row_dev = legendre.shape[2]
    grid_rows = field_grid.reshape(f_dev * lat_dev, lon_total)
    block_size = math.gcd(slot_total, 256)
    wave_blocks = wave_table.reshape(slot_total // block_size, block_size)

    def transform(wave_block):
        twiddle = twiddle_block(wave_block, lon_total)
        spectra = lax.dot_general(
            twiddle, grid_rows, (((1,), (1,)), ((), ())), preferred_element_type=jnp.float32
        )
        spectra = (spectra * (1.0 / lon_total)).astype(jnp.bfloat16)
        return jnp.transpose(spectra.reshape(2, block_size, f_dev, lat_dev), (1, 0, 2, 3))

    fourier = lax.map(transform, wave_blocks).reshape(slot_total, 2, f_dev, lat_dev)
    first_slot = lax.axis_index("lat") * slot_dev
    own_waves = lax.dynamic_slice_in_dim(wave_table, first_slot, slot_dev)
    trunc_total = 2 * row_dev * lax.axis_size("fld")
    row_index = lax.axis_index("fld") * row_dev + jnp.arange(row_dev, dtype=jnp.int32)
    parity = jnp.arange(2, dtype=jnp.int32)
    degree = own_waves[:, None, None] + 2 * row_index[None, :, None] + parity[None, None, :]
    valid_mask = (degree <= trunc_total - 1).astype(jnp.float32)
    regrouped = lax.all_to_all(fourier, "lat", split_axis=0, concat_axis=3, tiled=True)
    folded = fold_halves(regrouped)
    folded_piece = lax.all_gather(folded, "fld", axis=3, tiled=True)
    parts_count = folded_piece.shape[2]
    width = folded_piece.shape[3]
    merged = folded_piece.reshape(slot_dev, 2, parts_count * width, folded_piece.shape[4])
    coeffs = jnp.einsum("sprj,spcj->srpc", legendre, merged, preferred_element_type=jnp.float32)
    coeffs = coeffs.reshape(slot_dev, row_dev, 2, parts_count, width)
    coeffs = coeffs * valid_mask[:, :, :, None, None]
    return coeffs.reshape(slot_dev, row_dev, -1)


LANES = 128
HALF = 64
MESH = pl.DeviceIdType.MESH
ARRIVALS = (
    (1, 1, 0), (1, 2, 0), (0, 0, 0), (0, 0, 1), (0, 1, 0), (0, 2, 0),
    (1, 3, 0), (1, 1, 1), (1, 4, 0), (1, 2, 1), (1, 5, 0), (0, 3, 0),
    (0, 1, 1), (1, 6, 0), (0, 4, 0), (1, 3, 1), (0, 2, 1), (0, 5, 0),
    (1, 7, 0), (0, 6, 0), (1, 4, 1), (0, 3, 1), (1, 5, 1), (0, 7, 0),
    (1, 6, 1), (0, 4, 1), (1, 7, 1), (0, 5, 1), (0, 6, 1), (0, 7, 1),
)
STRAIGHT = ((4, 1), (5, 1))

def sin_cos_of_phase(phase, period):
    turns = jnp.floor(phase * (1.0 / period))
    rest = phase - turns * period
    rest = jnp.where(rest < 0, rest + period, rest)
    rest = jnp.where(rest >= period, rest - period, rest)
    eighth = period / 8
    q0 = rest < eighth
    q1 = rest < 3 * eighth
    q2 = rest < 5 * eighth
    q3 = rest < 7 * eighth
    centre = jnp.where(
        q0, 0.0, jnp.where(q1, 2 * eighth, jnp.where(q2, 4 * eighth, jnp.where(q3, 6 * eighth, period)))
    )
    x = (rest - centre) * (TWO_PI / period)
    y = x * x
    s = x * (1.0 + y * (-1 / 6 + y * (1 / 120 + y * (-1 / 5040 + y * (1 / 362880)))))
    c = 1.0 + y * (-1 / 2 + y * (1 / 24 + y * (-1 / 720 + y * (1 / 40320 - y * (1 / 3628800)))))
    even = q0 | (q2 & ~q1) | ~q3
    minus_sin = (q3 & ~q1)
    minus_cos = (q2 & ~q0)
    sine = jnp.where(even, s, c)
    sine = jnp.where(minus_sin, -sine, sine)
    cosine = jnp.where(even, c, s)
    cosine = jnp.where(minus_cos, -cosine, cosine)
    return sine, cosine


def transform_kernel(
    lat_count, wave_hbm, wave_row_hbm, field_ref, legendre_ref, out_ref,
    grid, twiddle, coarse, table, send, recv, folded, partial, spun, wave_smem, wave_row,
    field_sem, wave_sem, table_sem, sent, came,
):
    lat = lax.axis_index("lat")
    fld = lax.axis_index("fld")
    partner = fld + 1 - 2 * (fld % 2)
    core = fld % 2
    hub = fld + 1 - core
    hub_y = (hub + 2) % 4

    _, lat_dev, lon_total = field_ref.shape
    main = lat_dev // LANES
    tiles = 2 * main + 1
    slot_dev, _, row_dev, _ = legendre_ref.shape
    slot_total = wave_row_hbm.shape[1]
    half_lats = lat_count // 2
    chunk_tiles = ((0, 1), (1, main + 1), (main + 1, tiles))
    chunk_count = len(chunk_tiles)

    def band_of(index):
        south = index // half_lats
        return south, index + south * (lat_count - 1 - 2 * index)

    def place_of(index):
        south, band = band_of(index)
        return 2 * band + south

    south, band = band_of(lat)
    place = place_of(lat)
    odd = band % 2
    mixed = (south + odd) % 2

    def chunk_of(t):
        return [low <= t < high for low, high in chunk_tiles].index(True)

    def load(f, row, count, dst):
        pltpu.make_async_copy(
            field_ref.at[f, pl.ds(pl.multiple_of(row, HALF), count)],
            grid.at[pl.ds(pl.multiple_of(dst, HALF), count)],
            field_sem.at[chunk_of(load_tile[0])],
        ).start(priority=1)

    load_tile = [0]

    def load_main(f, t, dst_tile):
        load_tile[0] = dst_tile
        north_row = LANES * t + HALF * odd
        south_row = lat_dev - LANES - LANES * t - HALF * odd
        load(f, north_row + south * (south_row - north_row), LANES, LANES * dst_tile)

    wave_copies = [
        pltpu.make_async_copy(wave_row_hbm, wave_row, wave_sem.at[0]),
        pltpu.make_async_copy(wave_hbm, wave_smem, wave_sem.at[1]),
    ]
    for copy in wave_copies:
        copy.start()
    for t in range(main):
        load_main(0, t, t)
    load_tile[0] = main
    tail_row = (lat_dev - HALF) * (1 - mixed)
    load(0, tail_row, HALF, LANES * main + HALF * mixed)
    load(1, tail_row, HALF, LANES * main + HALF * (1 - mixed))
    for t in range(main):
        load_main(1, t, main + 1 + t)

    barrier = pltpu.get_barrier_semaphore()

    @pl.when(core == 1)
    def _():
        for d in range(1, lat_count):
            for c in range(2):
                pl.semaphore_signal(
                    barrier, inc=1, device_id=((lat + d) % lat_count, hub - c), device_id_type=MESH
                )
        pl.semaphore_signal(barrier, inc=1, device_id=(lat, hub_y), device_id_type=MESH)

    @pl.when(core == 0)
    def _():
        pl.semaphore_signal(barrier, inc=1, device_id=(lat, hub_y), device_id_type=MESH)

    pl.semaphore_signal(barrier, inc=1, device_id=(lat, partner), device_id_type=MESH)

    for copy in wave_copies:
        copy.wait()
    waves = wave_row[...].astype(jnp.float32)
    waves = jnp.concatenate([waves, waves], axis=1)
    width = 2 * slot_total
    coarse_count = lon_total // LANES
    k_fine = lax.broadcasted_iota(jnp.int32, (LANES, width), 0).astype(jnp.float32)
    is_sine = lax.broadcasted_iota(jnp.int32, (LANES, width), 1) >= slot_total
    quarter = jnp.where(is_sine, lon_total / 4, 0.0)
    fine_sin, fine_cos = sin_cos_of_phase(waves * k_fine + quarter, lon_total)
    coarse_rows = coarse.shape[1]
    k_coarse = lax.broadcasted_iota(jnp.int32, (coarse_rows, width), 0).astype(jnp.float32) * LANES
    coarse_sin, coarse_cos = sin_cos_of_phase(waves * k_coarse, lon_total)
    coarse[0] = coarse_sin
    coarse[1] = coarse_cos
    for a in range(coarse_count):
        block = coarse[1, pl.ds(a, 1), :] * fine_cos - coarse[0, pl.ds(a, 1), :] * fine_sin
        twiddle[pl.ds(a * LANES, LANES), :] = block.astype(jnp.bfloat16)

    row = lax.broadcasted_iota(jnp.int32, (LANES, LANES), 0)
    column = lax.broadcasted_iota(jnp.int32, (LANES, LANES), 1)
    turned = row + south * (LANES - 1 - 2 * row)
    order = (turned == column).astype(jnp.float32).astype(jnp.bfloat16)

    def flipped(d):
        index, bit = lat, 1
        while bit < lat_count:
            if d & bit:
                index = index + bit * (1 - 2 * ((lat // bit) % 2))
            bit *= 2
        return index

    def columns(q):
        low, high = chunk_tiles[q]
        return pl.ds(low * LANES, (high - low) * LANES)

    def remote(src, dst, sent_at, recv_at, device):
        return pltpu.make_async_remote_copy(
            src_ref=src, dst_ref=dst, send_sem=sent.at[sent_at], recv_sem=recv_at,
            device_id=device, device_id_type=MESH,
        )

    middle = (lat // 2 + lat // 4) % 2
    came_from = 2 * lat_count * 2

    def peer(e):
        index = flipped(e)
        if e < half_lats:
            return index, e
        turned = middle * (1 - 2 * ((index // 2) % 2))
        return index + 2 * turned, e + 2 * middle * (1 - 2 * ((e // 2) % 2))

    def lat_sem(c, d, q):
        return came.at[(c * lat_count + d) * 2 + (q == chunk_count - 1)]

    def y_sem(c, e, part):
        pair = e // 2
        split = pair + part * (half_lats // 2) if 2 * pair >= half_lats else pair
        return came.at[came_from + c * (half_lats + half_lats // 2) + split]

    def even_sem(h, group):
        return came.at[h * 4 + group]

    def part_columns(part):
        low = chunk_tiles[-1][0] if part else 0
        high = tiles if part else chunk_tiles[-1][0]
        return pl.ds(low * LANES, (high - low) * LANES)

    def pass_on(src, group, source_place, c, e, where, part=0):
        there = recv.at[group, source_place, :, where]
        remote(src, there, 1, y_sem(c, e, part), (lat, hub_y)).start()
        if (e, part) in STRAIGHT:
            remote(
                src, there, 1, even_sem(source_place // half_lats, group), (lat, hub_y - 1)
            ).start()
        remote(src, there, 2, even_sem(source_place // half_lats, group), (lat, partner)).start()

    def send_chunk(q):
        for e in range(lat_count - 1, 0, -1):
            owner, d = peer(e)
            remote(
                send.at[owner, :, columns(q)], recv.at[fld, place, :, columns(q)],
                0, lat_sem(core, d, q), (owner, hub),
            ).start()

        @pl.when(core == 1)
        def _():
            pass_on(send.at[lat, :, columns(q)], fld, place, 1, 0, columns(q))
            recv[fld, place, :, columns(q)] = send[lat, :, columns(q)]

        @pl.when(core == 0)
        def _():
            remote(
                send.at[lat, :, columns(q)], recv.at[fld, place, :, columns(q)],
                2, lat_sem(0, 0, q), (lat, partner),
            ).start()

    patience = jnp.maximum(chunk_count - 1 - (lat // 2 + lat % 2), 0)
    greeted = lat_count + 2 * core

    def release(q):
        @pl.when(patience == q)
        def _():
            pl.semaphore_wait(barrier, greeted)
            for k in range(q + 1):
                send_chunk(k)

        if q > 0:
            @pl.when(patience < q)
            def _():
                send_chunk(q)

    for q in range(chunk_count):
        low, high = chunk_tiles[q]
        rows = pl.ds(low * LANES, (high - low) * LANES)
        pltpu.make_async_copy(grid.at[rows], grid.at[rows], field_sem.at[q]).wait()
        spectra = jnp.dot(grid[rows, :], twiddle[...], preferred_element_type=jnp.float32)
        spectra = (spectra * (1.0 / lon_total)).astype(jnp.bfloat16)
        for t in range(low, high):
            part = spectra[(t - low) * LANES:(t - low + 1) * LANES, :]
            part = jnp.dot(order, part, preferred_element_type=jnp.float32)
            part = part.T
            for owner in range(lat_count):
                s0 = owner * slot_dev
                send[owner, :, pl.ds(t * LANES, LANES)] = jnp.concatenate(
                    [part[s0:s0 + slot_dev], part[slot_total + s0:slot_total + s0 + slot_dev]], axis=0
                ).astype(jnp.bfloat16)
        release(q)

    table_copy = pltpu.make_async_copy(legendre_ref, table, table_sem)
    table_copy.start()

    def relay(c, e, part):
        source, d = peer(e)
        group = hub - 1 + c
        source_place = place_of(source)
        here = recv.at[group, source_place, :, part_columns(part)]
        remote(here, here, 0, lat_sem(c, d, (chunk_count - 1) * part), (lat, partner)).wait_recv()
        pass_on(here, group, source_place, c, e, part_columns(part), part)

    def hand_over(c, pair, part=None):
        group = hub_y - 1 + c
        where = pl.ds(0, tiles * LANES) if part is None else part_columns(part)
        both = recv.at[group, pl.ds(0, 2), :, where]
        remote(both, both, 1, y_sem(c, 2 * pair, part or 0), (lat, hub_y)).wait_recv()
        for e in (2 * pair, 2 * pair + 1):
            if (e, part) not in STRAIGHT:
                source_place = place_of(peer(e)[0])
                there = recv.at[group, source_place, :, where]
                remote(
                    there, there, 2, even_sem(source_place // half_lats, group), (lat, partner)
                ).start()

    def gather(*parts):
        for pair, part in parts:
            for c in (1, 0):
                hand_over(c, pair, part)

    @pl.when(core == 1)
    def _():
        for c, e, part in ARRIVALS:
            relay(c, e, part)
        gather((0, None), (1, None), (2, 0), (3, 0), (2, 1))

    depth = 2 * slot_dev
    pair_lats = 2 * lat_dev
    low_half = lax.broadcasted_iota(jnp.int32, (depth, LANES), 1) < HALF
    total_rows = 8 * depth
    trunc_total = 2 * row_dev * 4
    slot_of = lax.broadcasted_iota(jnp.int32, (row_dev, total_rows), 1) % slot_dev
    degree_row = 2 * (lax.broadcasted_iota(jnp.int32, (row_dev, total_rows), 0) + fld * row_dev)
    wave_of = jnp.zeros((1, total_rows), jnp.int32)
    for s in range(slot_dev):
        wave_of = jnp.where(slot_of[:1] == s, wave_smem[lat * slot_dev + s], wave_of)
    table_copy.wait()
    for h in range(half_lats // 2 - 1, -1, -1):
        @pl.when(core == 0)
        def _():
            for group in range(4):
                block = recv.at[group, pl.ds(h * half_lats, half_lats)]
                remote(block, block, 2, even_sem(h, group), (lat, partner)).wait_recv()

        base = h * pair_lats
        for group in range(4):
            north = [recv[group, 2 * (2 * h + o)].astype(jnp.float32) for o in range(2)]
            mirror = [recv[group, 2 * (2 * h + o) + 1].astype(jnp.float32) for o in range(2)]
            for p in range(2):
                even_band, odd_band = [
                    n + m if p == 0 else n - m for n, m in zip(north, mirror)
                ]
                cut = main * LANES
                mid_even = even_band[:, cut:cut + LANES]
                mid_odd = odd_band[:, cut:cut + LANES]
                mid = (
                    jnp.where(low_half, mid_even, mid_odd),
                    pltpu.roll(jnp.where(low_half, mid_odd, mid_even), HALF, 1),
                )
                for f in range(2):
                    start = f * (cut + LANES)
                    rows = pl.ds((2 * group + f) * depth, depth)
                    folded[p, rows, pl.ds(base, cut)] = even_band[:, start:start + cut].astype(jnp.bfloat16)
                    folded[p, rows, pl.ds(base + cut, LANES)] = mid[f].astype(jnp.bfloat16)
                    folded[p, rows, pl.ds(base + cut + LANES, cut)] = odd_band[
                        :, start:start + cut
                    ].astype(jnp.bfloat16)
        for p in range(2):
            if h > 0 and p == 1:
                @pl.when(core == 1)
                def _():
                    gather((3, 1))
            kept = jnp.zeros((row_dev, total_rows), jnp.float32)
            for first in range(0, slot_dev, 2):
                sums = lax.dot_general(
                    table[first:first + 2, p, :, pl.ds(base, pair_lats)].reshape(2 * row_dev, pair_lats),
                    folded[p, :, pl.ds(base, pair_lats)],
                    (((1,), (1,)), ((), ())), preferred_element_type=jnp.float32,
                )
                for s in range(2):
                    kept = jnp.where(slot_of == first + s, sums[s * row_dev:(s + 1) * row_dev], kept)
            if h > 0:
                partial[p] = kept
                continue
            kept = jnp.where(degree_row + (wave_of + p) <= trunc_total - 1, kept + partial[p], 0.0)
            padded = jnp.concatenate(
                [kept, jnp.zeros((spun.shape[1] * LANES - row_dev, total_rows), jnp.float32)], axis=0
            )
            for t in range(spun.shape[1]):
                spun[p, t] = padded[t * LANES:(t + 1) * LANES].T
    for s in range(slot_dev):
        for p in range(2):
            for c in range(2):
                for t in range(spun.shape[1]):
                    kept_rows = min(LANES, row_dev - t * LANES)
                    out_ref[s, pl.ds(p * 16 + c * 8, 8), pl.ds(t * LANES, kept_rows)] = spun[
                        p, t, pl.ds(c * slot_dev + s, 8, stride=depth), :
                    ][:, :kept_rows]
    def drain(kind, block):
        remote(block, block, kind, table_sem, (lat, partner)).wait_send()

    drain(0, recv.at[fld, pl.ds(0, lat_count - 1)])

    @pl.when(core == 1)
    def _():
        straight = 2 * len(STRAIGHT)
        drain(1, recv.at[pl.ds(0, 2)])
        drain(2, recv.at[pl.ds(0, 3)])
        if straight:
            drain(1, recv.at[0, pl.ds(0, straight), :, part_columns(1)])
        if straight < lat_count:
            drain(2, recv.at[0, pl.ds(straight, lat_count - straight), :, part_columns(1)])
        drain(2, recv.at[0, :, :, part_columns(0)])

    @pl.when(core == 0)
    def _():
        drain(2, recv.at[0, 0])


def shards_by_kernel(field_grid, wave_table, legendre):
    f_dev, lat_dev, lon_total = field_grid.shape
    slot_dev, _, row_dev, north_total = legendre.shape
    slot_total = wave_table.shape[0]
    lat_count = lax.axis_size("lat")
    rows = f_dev * lat_dev
    bf16, f32 = jnp.bfloat16, jnp.float32
    dma = pltpu.SemaphoreType.DMA
    padded_rows = -(-row_dev // LANES) * LANES
    coarse_rows = -(-(lon_total // LANES) // 8) * 8
    vmem, smem = pltpu.VMEM, pltpu.SMEM
    out = pl.pallas_call(
        functools.partial(transform_kernel, lat_count),
        out_shape=pltpu.VMEM((slot_dev, 32, row_dev), f32),
        in_specs=[pl.BlockSpec(memory_space=pl.ANY)] * 4,
        out_specs=pl.BlockSpec(memory_space=vmem),
        scratch_shapes=[
            vmem((rows, lon_total), bf16),
            vmem((lon_total, 2 * slot_total), bf16),
            vmem((2, coarse_rows, 2 * slot_total), f32),
            vmem(legendre.shape, bf16),
            vmem((lat_count, 2 * slot_dev, rows), bf16),
            vmem((4, lat_count, 2 * slot_dev, rows), bf16),
            vmem((2, 16 * slot_dev, north_total), bf16),
            vmem((2, row_dev, 16 * slot_dev), f32),
            vmem((2, padded_rows // LANES, 16 * slot_dev, LANES), f32),
            smem((slot_total,), jnp.int32),
            vmem((1, slot_total), jnp.int32),
            dma((3,)),
            dma((2,)),
            dma(()),
            dma((3,)),
            dma((5 * lat_count + lat_count // 2,)),
        ],
        compiler_params=pltpu.CompilerParams(
            collective_id=0, has_side_effects=True
        ),
    )(wave_table, wave_table.reshape(1, slot_total), field_grid, legendre)
    return jnp.transpose(out, (0, 2, 1))


def shards(field_grid, wave_table, legendre):
    f_dev, lat_dev, lon_total = field_grid.shape
    slot_dev, _, row_dev, _ = legendre.shape
    slot_total = wave_table.shape[0]
    fits = (
        f_dev == 2
        and slot_dev == 8
        and 2 * slot_total == LANES
        and lat_dev % LANES == HALF
        and lat_dev > LANES
        and lax.axis_size("fld") == 4
        and lax.axis_size("lat") == 8
        and lon_total % LANES == 0
        and row_dev % 8 == 0
        and 2 * row_dev * 4 * lon_total < 2**24
    )
    if fits:
        return shards_by_kernel(field_grid, wave_table, legendre)
    return shards_by_collectives(field_grid, wave_table, legendre)


def solution(mesh):
    placed = (P("fld", "lat", None), P(), P("lat", None, "fld", None))
    return jax.shard_map(
        shards, mesh=mesh, in_specs=placed, out_specs=P("lat", "fld", None), check_vma=False
    )
```

```python
import functools
import math

import jax
import jax.numpy as jnp
from jax import lax
from jax.experimental import pallas as pl
from jax.experimental.pallas import tpu as pltpu
from jax.sharding import PartitionSpec as P

TWO_PI = 2.0 * math.pi


def twiddle_block(wave_block, lon_total):
    fine_count = math.gcd(lon_total, 128)
    coarse_count = lon_total // fine_count
    waves = wave_block[:, None]
    coarse_index = (
        waves * (jnp.arange(coarse_count, dtype=jnp.int32) * fine_count)[None, :] % lon_total
    )
    fine_index = waves * jnp.arange(fine_count, dtype=jnp.int32)[None, :] % lon_total
    coarse_angle = coarse_index.astype(jnp.float32) * (TWO_PI / lon_total)
    fine_angle = fine_index.astype(jnp.float32) * (TWO_PI / lon_total)
    coarse_cos = jnp.cos(coarse_angle)[:, :, None]
    coarse_sin = jnp.sin(coarse_angle)[:, :, None]
    fine_cos = jnp.cos(fine_angle)[:, None, :]
    fine_sin = jnp.sin(fine_angle)[:, None, :]
    cosine = (coarse_cos * fine_cos - coarse_sin * fine_sin).reshape(wave_block.shape[0], lon_total)
    minus_sine = (-(coarse_sin * fine_cos + coarse_cos * fine_sin)).reshape(
        wave_block.shape[0], lon_total
    )
    return jnp.concatenate([cosine, minus_sine], axis=0).astype(jnp.bfloat16)


def fold_halves(fourier):
    half_lat = fourier.shape[-1] // 2
    north_rows = fourier[..., :half_lat].astype(jnp.float32)
    south_rows = jnp.flip(fourier[..., half_lat:], axis=-1).astype(jnp.float32)
    return jnp.stack([north_rows + south_rows, north_rows - south_rows], axis=1).astype(
        jnp.bfloat16
    )


def shards_by_collectives(field_grid, wave_table, legendre):
    f_dev, lat_dev, lon_total = field_grid.shape
    slot_total = wave_table.shape[0]
    slot_dev = legendre.shape[0]
    row_dev = legendre.shape[2]
    grid_rows = field_grid.reshape(f_dev * lat_dev, lon_total)
    block_size = math.gcd(slot_total, 256)
    wave_blocks = wave_table.reshape(slot_total // block_size, block_size)

    def transform(wave_block):
        twiddle = twiddle_block(wave_block, lon_total)
        spectra = lax.dot_general(
            twiddle, grid_rows, (((1,), (1,)), ((), ())), preferred_element_type=jnp.float32
        )
        spectra = (spectra * (1.0 / lon_total)).astype(jnp.bfloat16)
        return jnp.transpose(spectra.reshape(2, block_size, f_dev, lat_dev), (1, 0, 2, 3))

    fourier = lax.map(transform, wave_blocks).reshape(slot_total, 2, f_dev, lat_dev)
    first_slot = lax.axis_index("lat") * slot_dev
    own_waves = lax.dynamic_slice_in_dim(wave_table, first_slot, slot_dev)
    trunc_total = 2 * row_dev * lax.axis_size("fld")
    row_index = lax.axis_index("fld") * row_dev + jnp.arange(row_dev, dtype=jnp.int32)
    parity = jnp.arange(2, dtype=jnp.int32)
    degree = own_waves[:, None, None] + 2 * row_index[None, :, None] + parity[None, None, :]
    valid_mask = (degree <= trunc_total - 1).astype(jnp.float32)
    regrouped = lax.all_to_all(fourier, "lat", split_axis=0, concat_axis=3, tiled=True)
    folded = fold_halves(regrouped)
    folded_piece = lax.all_gather(folded, "fld", axis=3, tiled=True)
    parts_count = folded_piece.shape[2]
    width = folded_piece.shape[3]
    merged = folded_piece.reshape(slot_dev, 2, parts_count * width, folded_piece.shape[4])
    coeffs = jnp.einsum("sprj,spcj->srpc", legendre, merged, preferred_element_type=jnp.float32)
    coeffs = coeffs.reshape(slot_dev, row_dev, 2, parts_count, width)
    coeffs = coeffs * valid_mask[:, :, :, None, None]
    return coeffs.reshape(slot_dev, row_dev, -1)


LANES = 128
HALF = 64
MESH = pl.DeviceIdType.MESH
ARRIVALS = (
    (1, 1, 0), (1, 2, 0), (0, 0, 0), (0, 0, 1), (0, 1, 0), (1, 3, 0),
    (1, 4, 0), (1, 1, 1), (0, 2, 0), (1, 2, 1), (0, 3, 0), (1, 5, 0),
    (0, 1, 1), (1, 6, 0), (0, 2, 1), (1, 3, 1), (0, 4, 0), (1, 4, 1),
    (0, 5, 0), (0, 3, 1), (0, 6, 0), (1, 7, 0), (1, 6, 1), (1, 5, 1),
    (0, 4, 1), (0, 7, 0), (0, 6, 1), (1, 7, 1), (0, 5, 1), (0, 7, 1),
)
STRAIGHT = ()

def sin_cos_of_phase(phase, period):
    turns = jnp.floor(phase * (1.0 / period))
    rest = phase - turns * period
    rest = jnp.where(rest < 0, rest + period, rest)
    rest = jnp.where(rest >= period, rest - period, rest)
    eighth = period / 8
    q0 = rest < eighth
    q1 = rest < 3 * eighth
    q2 = rest < 5 * eighth
    q3 = rest < 7 * eighth
    centre = jnp.where(
        q0, 0.0, jnp.where(q1, 2 * eighth, jnp.where(q2, 4 * eighth, jnp.where(q3, 6 * eighth, period)))
    )
    x = (rest - centre) * (TWO_PI / period)
    y = x * x
    s = x * (1.0 + y * (-1 / 6 + y * (1 / 120 + y * (-1 / 5040 + y * (1 / 362880)))))
    c = 1.0 + y * (-1 / 2 + y * (1 / 24 + y * (-1 / 720 + y * (1 / 40320 - y * (1 / 3628800)))))
    even = q0 | (q2 & ~q1) | ~q3
    minus_sin = (q3 & ~q1)
    minus_cos = (q2 & ~q0)
    sine = jnp.where(even, s, c)
    sine = jnp.where(minus_sin, -sine, sine)
    cosine = jnp.where(even, c, s)
    cosine = jnp.where(minus_cos, -cosine, cosine)
    return sine, cosine


def transform_kernel(
    lat_count, wave_hbm, wave_row_hbm, field_ref, legendre_ref, out_ref,
    grid, twiddle, coarse, table, send, recv, folded, partial, spun, wave_smem, wave_row,
    field_sem, wave_sem, table_sem, sent, came,
):
    lat = lax.axis_index("lat")
    fld = lax.axis_index("fld")
    partner = fld + 1 - 2 * (fld % 2)
    core = fld % 2
    hub = fld + 1 - core
    hub_y = (hub + 2) % 4
    side = fld // 2
    first_chip = (lat == 0) & (side == 0)
    across = (lat == 0) & (side == 1)
    far = (lat >= lat_count // 2) & (fld == 2)

    _, lat_dev, lon_total = field_ref.shape
    main = lat_dev // LANES
    tiles = 2 * main + 1
    slot_dev, _, row_dev, _ = legendre_ref.shape
    slot_total = wave_row_hbm.shape[1]
    half_lats = lat_count // 2
    chunk_tiles = ((0, 1), (1, main + 1), (main + 1, tiles))
    chunk_count = len(chunk_tiles)

    def band_of(index):
        south = index // half_lats
        return south, index + south * (lat_count - 1 - 2 * index)

    def place_of(index):
        south, band = band_of(index)
        return 2 * band + south

    south, band = band_of(lat)
    place = place_of(lat)
    odd = band % 2
    mixed = (south + odd) % 2

    def chunk_of(t):
        return [low <= t < high for low, high in chunk_tiles].index(True)

    def load(f, row, count, dst):
        pltpu.make_async_copy(
            field_ref.at[f, pl.ds(pl.multiple_of(row, HALF), count)],
            grid.at[pl.ds(pl.multiple_of(dst, HALF), count)],
            field_sem.at[chunk_of(load_tile[0])],
        ).start(priority=1)

    load_tile = [0]

    def load_main(f, t, dst_tile):
        load_tile[0] = dst_tile
        north_row = LANES * t + HALF * odd
        south_row = lat_dev - LANES - LANES * t - HALF * odd
        load(f, north_row + south * (south_row - north_row), LANES, LANES * dst_tile)

    wave_copies = [
        pltpu.make_async_copy(wave_row_hbm, wave_row, wave_sem.at[0]),
        pltpu.make_async_copy(wave_hbm, wave_smem, wave_sem.at[1]),
    ]
    for copy in wave_copies:
        copy.start()
    for t in range(main):
        load_main(0, t, t)
    load_tile[0] = main
    tail_row = (lat_dev - HALF) * (1 - mixed)
    load(0, tail_row, HALF, LANES * main + HALF * mixed)
    load(1, tail_row, HALF, LANES * main + HALF * (1 - mixed))
    for t in range(main):
        load_main(1, t, main + 1 + t)

    barrier = pltpu.get_barrier_semaphore()

    @pl.when(core == 1)
    def _():
        for d in range(1, lat_count):
            for c in range(2):
                pl.semaphore_signal(
                    barrier, inc=1, device_id=((lat + d) % lat_count, hub - c), device_id_type=MESH
                )
        pl.semaphore_signal(barrier, inc=1, device_id=(lat, hub_y), device_id_type=MESH)

    @pl.when(core == 0)
    def _():
        pl.semaphore_signal(barrier, inc=1, device_id=(lat, hub_y), device_id_type=MESH)

    pl.semaphore_signal(barrier, inc=1, device_id=(lat, partner), device_id_type=MESH)

    @pl.when(first_chip & (core == 1))
    def _():
        for other in range(half_lats, lat_count):
            pl.semaphore_signal(barrier, inc=1, device_id=(other, 2), device_id_type=MESH)

    for copy in wave_copies:
        copy.wait()
    waves = wave_row[...].astype(jnp.float32)
    waves = jnp.concatenate([waves, waves], axis=1)
    width = 2 * slot_total
    coarse_count = lon_total // LANES
    k_fine = lax.broadcasted_iota(jnp.int32, (LANES, width), 0).astype(jnp.float32)
    is_sine = lax.broadcasted_iota(jnp.int32, (LANES, width), 1) >= slot_total
    quarter = jnp.where(is_sine, lon_total / 4, 0.0)
    fine_sin, fine_cos = sin_cos_of_phase(waves * k_fine + quarter, lon_total)
    coarse_rows = coarse.shape[1]
    k_coarse = lax.broadcasted_iota(jnp.int32, (coarse_rows, width), 0).astype(jnp.float32) * LANES
    coarse_sin, coarse_cos = sin_cos_of_phase(waves * k_coarse, lon_total)
    coarse[0] = coarse_sin
    coarse[1] = coarse_cos
    for a in range(coarse_count):
        block = coarse[1, pl.ds(a, 1), :] * fine_cos - coarse[0, pl.ds(a, 1), :] * fine_sin
        twiddle[pl.ds(a * LANES, LANES), :] = block.astype(jnp.bfloat16)

    row = lax.broadcasted_iota(jnp.int32, (LANES, LANES), 0)
    column = lax.broadcasted_iota(jnp.int32, (LANES, LANES), 1)
    turned = row + south * (LANES - 1 - 2 * row)
    order = (turned == column).astype(jnp.float32).astype(jnp.bfloat16)

    def flipped(d):
        index, bit = lat, 1
        while bit < lat_count:
            if d & bit:
                index = index + bit * (1 - 2 * ((lat // bit) % 2))
            bit *= 2
        return index

    def columns(q):
        low, high = chunk_tiles[q]
        return pl.ds(low * LANES, (high - low) * LANES)

    def remote(src, dst, sent_at, recv_at, device):
        return pltpu.make_async_remote_copy(
            src_ref=src, dst_ref=dst, send_sem=sent.at[sent_at], recv_sem=recv_at,
            device_id=device, device_id_type=MESH,
        )

    middle = (lat // 2 + lat // 4) % 2
    came_from = 4 * lat_count - 2

    def peer(e):
        index = flipped(e)
        if e < half_lats:
            return index, e
        turned = middle * (1 - 2 * ((index // 2) % 2))
        return index + 2 * turned, e + 2 * middle * (1 - 2 * ((e // 2) % 2))

    def lat_sem(c, d, q):
        return came.at[(c * (lat_count - 1) + d) * 2 + (q == chunk_count - 1)]

    def y_sem(c, e, part):
        if isinstance(e, int) and e < half_lats:
            split = 0
        else:
            split = e // 2 - half_lats // 2 + 1 + 2 * part
        return came.at[came_from + c * 5 + split]

    def even_sem(source_place, part, group):
        if part == 0:
            return came.at[group]
        return came.at[4 * (1 - source_place // half_lats) + group]

    def part_columns(part):
        low = chunk_tiles[-1][0] if part else 0
        high = tiles if part else chunk_tiles[-1][0]
        return pl.ds(low * LANES, (high - low) * LANES)

    def straight_from_source(c, e, part):
        return c == 0 and e >= half_lats and part == 1

    def unless(skipped, chip, action):
        if skipped:
            pl.when(jnp.logical_not(chip))(action)
        else:
            action()

    def pass_on(src, group, source_place, c, e, where, part=0):
        there = recv.at[group, source_place, :, where]

        def cross():
            remote(src, there, 1, y_sem(c, e, part * (e >= half_lats)), (lat, hub_y)).start()
            if (c, e, part) in STRAIGHT:
                remote(
                    src, there, 1, even_sem(source_place, part, group), (lat, hub_y - 1)
                ).start()

        unless(straight_from_source(c, e, part), across, cross)
        remote(src, there, 2, even_sem(source_place, part, group), (lat, partner)).start()

    def send_chunk(q):
        for e in range(lat_count - 1, 0, -1):
            owner, d = peer(e)
            remote(
                send.at[owner, :, columns(q)], recv.at[fld, place, :, columns(q)],
                0, lat_sem(core, d, q), (owner, hub),
            ).start()

        if q == chunk_count - 1:
            @pl.when(far)
            def _():
                block = recv.at[fld, place, :, columns(q)]
                remote(send.at[0, :, columns(q)], block, 0, y_sem(0, lat, 1), (0, 1)).start()

        @pl.when(core == 1)
        def _():
            pass_on(send.at[lat, :, columns(q)], fld, place, 1, 0, columns(q), int(q == chunk_count - 1))
            recv[fld, place, :, columns(q)] = send[lat, :, columns(q)]

        @pl.when(core == 0)
        def _():
            remote(
                send.at[lat, :, columns(q)], recv.at[fld, place, :, columns(q)],
                2, lat_sem(0, 0, q), (lat, partner),
            ).start()

    patience = jnp.maximum(chunk_count - 1 - (lat // 2 + lat % 2), 0)
    greeted = lat_count + 2 * core + far.astype(jnp.int32)

    def release(q):
        @pl.when(patience == q)
        def _():
            pl.semaphore_wait(barrier, greeted)
            for k in range(q + 1):
                send_chunk(k)

        if q > 0:
            @pl.when(patience < q)
            def _():
                send_chunk(q)

    for q in range(chunk_count):
        low, high = chunk_tiles[q]
        rows = pl.ds(low * LANES, (high - low) * LANES)
        pltpu.make_async_copy(grid.at[rows], grid.at[rows], field_sem.at[q]).wait()
        spectra = jnp.dot(grid[rows, :], twiddle[...], preferred_element_type=jnp.float32)
        spectra = (spectra * (1.0 / lon_total)).astype(jnp.bfloat16)
        for t in range(low, high):
            part = spectra[(t - low) * LANES:(t - low + 1) * LANES, :]
            part = jnp.dot(order, part, preferred_element_type=jnp.float32)
            part = part.T
            for owner in range(lat_count):
                s0 = owner * slot_dev
                send[owner, :, pl.ds(t * LANES, LANES)] = jnp.concatenate(
                    [part[s0:s0 + slot_dev], part[slot_total + s0:slot_total + s0 + slot_dev]], axis=0
                ).astype(jnp.bfloat16)
        release(q)

    cut = main * LANES
    pair_lats = 2 * lat_dev
    spans = (
        (cut, 0, LANES),
        (pair_lats, LANES, pair_lats),
        (0, pair_lats + LANES, cut),
        (cut + LANES, pair_lats + LANES + cut, cut),
    )
    for source, target, count in spans:
        pltpu.make_async_copy(
            legendre_ref.at[:, :, :, pl.ds(source, count)],
            table.at[:, :, :, pl.ds(target, count)], table_sem,
        ).start()

    def relay(c, e, part):
        source, d = peer(e)
        group = hub - 1 + c
        source_place = place_of(source)
        here = recv.at[group, source_place, :, part_columns(part)]
        remote(here, here, 0, lat_sem(c, d, (chunk_count - 1) * part), (lat, partner)).wait_recv()
        pass_on(here, group, source_place, c, e, part_columns(part), part)

    def hand_over(c, pair, part=None):
        group = hub_y - 1 + c
        where = pl.ds(0, tiles * LANES) if part is None else part_columns(part)
        members = range(half_lats) if pair == 0 else (2 * pair, 2 * pair + 1)
        both = recv.at[group, pl.ds(0, len(members)), :, where]
        remote(both, both, 1, y_sem(c, 2 * pair, part or 0), (lat, hub_y)).wait_recv()
        for e in members:
            source_place = place_of(peer(e)[0])
            for k in (0, 1) if part is None else (part,):
                if (c, e, k) in STRAIGHT:
                    continue
                there = recv.at[group, source_place, :, part_columns(k)]
                hand = remote(there, there, 2, even_sem(source_place, k, group), (lat, partner))
                hand.start()

    def gather(*parts):
        for c, pair, part in parts:
            hand_over(c, pair, part)

    @pl.when(core == 1)
    def _():
        for c, e, part in ARRIVALS:
            relay(c, e, part)
        gather(
            (1, 2, 0), (0, 2, 0), (1, 0, None), (0, 0, None), (1, 3, 0), (1, 2, 1),
            (0, 3, 0), (0, 2, 1),
        )

    depth = 2 * slot_dev
    low_half = lax.broadcasted_iota(jnp.int32, (depth, LANES), 1) < HALF
    total_rows = 8 * depth
    trunc_total = 2 * row_dev * 4
    slot_of = lax.broadcasted_iota(jnp.int32, (row_dev, total_rows), 1) % slot_dev
    degree_row = 2 * (lax.broadcasted_iota(jnp.int32, (row_dev, total_rows), 0) + fld * row_dev)
    wave_of = jnp.zeros((1, total_rows), jnp.int32)
    for s in range(slot_dev):
        wave_of = jnp.where(slot_of[:1] == s, wave_smem[lat * slot_dev + s], wave_of)
    pltpu.make_async_copy(table, table, table_sem).wait()
    widths = (pair_lats + LANES, 2 * cut)

    def fold(h, keep):
        for group in range(4):
            north = [recv[group, 2 * (2 * h + o), :, keep].astype(jnp.float32) for o in range(2)]
            mirror = [recv[group, 2 * (2 * h + o) + 1, :, keep].astype(jnp.float32) for o in range(2)]
            for p in range(2):
                yield group, p, [n + m if p == 0 else n - m for n, m in zip(north, mirror)]

    def put(group, p, f, start, value):
        rows = pl.ds((2 * group + f) * depth, depth)
        folded[p, rows, pl.ds(start, value.shape[1])] = value.astype(jnp.bfloat16)

    def put_middle(group, p, bands, start):
        mid_even, mid_odd = bands
        put(group, p, 0, start, jnp.where(low_half, mid_even, mid_odd))
        put(
            group, p, 1, start,
            pltpu.roll(jnp.where(low_half, mid_odd, mid_even), HALF, 1),
        )

    for phase in range(2):
        base = phase * widths[0]
        @pl.when(core == 0)
        def _():
            for group in range(4):
                if phase == 0:
                    block = recv.at[group, :, :, pl.ds(0, (tiles + main + 1) // 2 * LANES)]
                else:
                    block = recv.at[group, pl.ds(0, half_lats), :, part_columns(1)]
                remote(block, block, 2, came.at[4 * phase + group], (lat, partner)).wait_recv()

        if phase == 0:
            for group, p, bands in fold(0, pl.ds(cut, LANES)):
                put_middle(group, p, bands, 0)
            for group, p, (even_band, odd_band) in fold(1, slice(None)):
                for f in range(2):
                    start = f * (cut + LANES)
                    put(group, p, f, LANES, even_band[:, start:start + cut])
                    put(group, p, f, LANES + cut + LANES, odd_band[:, start:start + cut])
                put_middle(
                    group, p, [band[:, cut:cut + LANES] for band in (even_band, odd_band)], LANES + cut
                )
        else:
            for f in range(2):
                for group, p, bands in fold(0, pl.ds(f * (cut + LANES), cut)):
                    for o in range(2):
                        put(group, p, f, base + o * cut, bands[o])
        for p in range(2):
            if phase == 0 and p == 1:
                @pl.when(core == 1)
                def _():
                    gather((1, 3, 1), (0, 3, 1))

            kept = jnp.zeros((row_dev, total_rows), jnp.float32)
            for first in range(0, slot_dev, 2):
                sums = lax.dot_general(
                    table[first:first + 2, p, :, pl.ds(base, widths[phase])].reshape(
                        2 * row_dev, widths[phase]
                    ),
                    folded[p, :, pl.ds(base, widths[phase])],
                    (((1,), (1,)), ((), ())), preferred_element_type=jnp.float32,
                )
                for s in range(2):
                    kept = jnp.where(slot_of == first + s, sums[s * row_dev:(s + 1) * row_dev], kept)
            if phase == 0:
                partial[p] = kept
                continue
            kept = jnp.where(degree_row + (wave_of + p) <= trunc_total - 1, kept + partial[p], 0.0)
            padded = jnp.concatenate(
                [kept, jnp.zeros((spun.shape[1] * LANES - row_dev, total_rows), jnp.float32)], axis=0
            )
            for t in range(spun.shape[1]):
                spun[p, t] = padded[t * LANES:(t + 1) * LANES].T
    for s in range(slot_dev):
        for p in range(2):
            for c in range(2):
                for t in range(spun.shape[1]):
                    kept_rows = min(LANES, row_dev - t * LANES)
                    out_ref[s, pl.ds(p * 16 + c * 8, 8), pl.ds(t * LANES, kept_rows)] = spun[
                        p, t, pl.ds(c * slot_dev + s, 8, stride=depth), :
                    ][:, :kept_rows]
    def drain(kind, block):
        remote(block, block, kind, table_sem, (lat, partner)).wait_send()

    drain(0, recv.at[fld, pl.ds(0, lat_count - 1)])

    @pl.when(far)
    def _():
        drain(0, recv.at[0, 0, :, part_columns(1)])

    @pl.when(core == 1)
    def _():
        def drain_parts(kind, chip, events):
            for part in range(2):
                where = part_columns(part)
                skipped = [v for v in events if v[2] == part and straight_from_source(*v)]
                others = skipped if chip is not None else []
                always = [v for v in events if v[2] == part and v not in others]
                for start in range(0, len(always), lat_count):
                    count = min(lat_count, len(always) - start)
                    drain(kind, recv.at[0, pl.ds(0, count), :, where])
                if others:
                    @pl.when(jnp.logical_not(chip))
                    def _():
                        drain(kind, recv.at[0, pl.ds(0, len(others)), :, where])

        pieces = [(c, e, part) for c in range(2) for e in range(lat_count) for part in range(2)]
        drain_parts(1, across, pieces + list(STRAIGHT))
        drain(2, recv.at[pl.ds(0, 2)])
        drain_parts(2, None, [v for v in pieces if v not in STRAIGHT])

    @pl.when(core == 0)
    def _():
        drain(2, recv.at[0, 0])


def shards_by_kernel(field_grid, wave_table, legendre):
    f_dev, lat_dev, lon_total = field_grid.shape
    slot_dev, _, row_dev, north_total = legendre.shape
    slot_total = wave_table.shape[0]
    lat_count = lax.axis_size("lat")
    rows = f_dev * lat_dev
    bf16, f32 = jnp.bfloat16, jnp.float32
    dma = pltpu.SemaphoreType.DMA
    padded_rows = -(-row_dev // LANES) * LANES
    coarse_rows = -(-(lon_total // LANES) // 8) * 8
    vmem, smem = pltpu.VMEM, pltpu.SMEM
    out = pl.pallas_call(
        functools.partial(transform_kernel, lat_count),
        out_shape=pltpu.VMEM((slot_dev, 32, row_dev), f32),
        in_specs=[pl.BlockSpec(memory_space=pl.ANY)] * 4,
        out_specs=pl.BlockSpec(memory_space=vmem),
        scratch_shapes=[
            vmem((rows, lon_total), bf16),
            vmem((lon_total, 2 * slot_total), bf16),
            vmem((2, coarse_rows, 2 * slot_total), f32),
            vmem(legendre.shape, bf16),
            vmem((lat_count, 2 * slot_dev, rows), bf16),
            vmem((4, lat_count, 2 * slot_dev, rows), bf16),
            vmem((2, 16 * slot_dev, north_total), bf16),
            vmem((2, row_dev, 16 * slot_dev), f32),
            vmem((2, padded_rows // LANES, 16 * slot_dev, LANES), f32),
            smem((slot_total,), jnp.int32),
            vmem((1, slot_total), jnp.int32),
            dma((3,)),
            dma((2,)),
            dma(()),
            dma((3,)),
            dma((4 * lat_count + 8,)),
        ],
        compiler_params=pltpu.CompilerParams(
            collective_id=0, has_side_effects=True
        ),
    )(wave_table, wave_table.reshape(1, slot_total), field_grid, legendre)
    return jnp.transpose(out, (0, 2, 1))


def shards(field_grid, wave_table, legendre):
    f_dev, lat_dev, lon_total = field_grid.shape
    slot_dev, _, row_dev, _ = legendre.shape
    slot_total = wave_table.shape[0]
    fits = (
        f_dev == 2
        and slot_dev == 8
        and 2 * slot_total == LANES
        and lat_dev % LANES == HALF
        and lat_dev // LANES % 2 == 0
        and lat_dev > LANES
        and lax.axis_size("fld") == 4
        and lax.axis_size("lat") == 8
        and lon_total % LANES == 0
        and row_dev % 8 == 0
        and 2 * row_dev * 4 * lon_total < 2**24
    )
    if fits:
        return shards_by_kernel(field_grid, wave_table, legendre)
    return shards_by_collectives(field_grid, wave_table, legendre)


def solution(mesh):
    placed = (P("fld", "lat", None), P(), P("lat", None, "fld", None))
    return jax.shard_map(
        shards, mesh=mesh, in_specs=placed, out_specs=P("lat", "fld", None), check_vma=False
    )
```

```python
import functools
import math

import jax
import jax.numpy as jnp
from jax import lax
from jax.experimental import pallas as pl
from jax.experimental.pallas import tpu as pltpu
from jax.sharding import PartitionSpec as P

TWO_PI = 2.0 * math.pi


def twiddle_block(wave_block, lon_total):
    fine_count = math.gcd(lon_total, 128)
    coarse_count = lon_total // fine_count
    waves = wave_block[:, None]
    coarse_index = (
        waves * (jnp.arange(coarse_count, dtype=jnp.int32) * fine_count)[None, :] % lon_total
    )
    fine_index = waves * jnp.arange(fine_count, dtype=jnp.int32)[None, :] % lon_total
    coarse_angle = coarse_index.astype(jnp.float32) * (TWO_PI / lon_total)
    fine_angle = fine_index.astype(jnp.float32) * (TWO_PI / lon_total)
    coarse_cos = jnp.cos(coarse_angle)[:, :, None]
    coarse_sin = jnp.sin(coarse_angle)[:, :, None]
    fine_cos = jnp.cos(fine_angle)[:, None, :]
    fine_sin = jnp.sin(fine_angle)[:, None, :]
    cosine = (coarse_cos * fine_cos - coarse_sin * fine_sin).reshape(wave_block.shape[0], lon_total)
    minus_sine = (-(coarse_sin * fine_cos + coarse_cos * fine_sin)).reshape(
        wave_block.shape[0], lon_total
    )
    return jnp.concatenate([cosine, minus_sine], axis=0).astype(jnp.bfloat16)


def fold_halves(fourier):
    half_lat = fourier.shape[-1] // 2
    north_rows = fourier[..., :half_lat].astype(jnp.float32)
    south_rows = jnp.flip(fourier[..., half_lat:], axis=-1).astype(jnp.float32)
    return jnp.stack([north_rows + south_rows, north_rows - south_rows], axis=1).astype(
        jnp.bfloat16
    )


def shards_by_collectives(field_grid, wave_table, legendre):
    f_dev, lat_dev, lon_total = field_grid.shape
    slot_total = wave_table.shape[0]
    slot_dev = legendre.shape[0]
    row_dev = legendre.shape[2]
    grid_rows = field_grid.reshape(f_dev * lat_dev, lon_total)
    block_size = math.gcd(slot_total, 256)
    wave_blocks = wave_table.reshape(slot_total // block_size, block_size)

    def transform(wave_block):
        twiddle = twiddle_block(wave_block, lon_total)
        spectra = lax.dot_general(
            twiddle, grid_rows, (((1,), (1,)), ((), ())), preferred_element_type=jnp.float32
        )
        spectra = (spectra * (1.0 / lon_total)).astype(jnp.bfloat16)
        return jnp.transpose(spectra.reshape(2, block_size, f_dev, lat_dev), (1, 0, 2, 3))

    fourier = lax.map(transform, wave_blocks).reshape(slot_total, 2, f_dev, lat_dev)
    first_slot = lax.axis_index("lat") * slot_dev
    own_waves = lax.dynamic_slice_in_dim(wave_table, first_slot, slot_dev)
    trunc_total = 2 * row_dev * lax.axis_size("fld")
    row_index = lax.axis_index("fld") * row_dev + jnp.arange(row_dev, dtype=jnp.int32)
    parity = jnp.arange(2, dtype=jnp.int32)
    degree = own_waves[:, None, None] + 2 * row_index[None, :, None] + parity[None, None, :]
    valid_mask = (degree <= trunc_total - 1).astype(jnp.float32)
    regrouped = lax.all_to_all(fourier, "lat", split_axis=0, concat_axis=3, tiled=True)
    folded = fold_halves(regrouped)
    folded_piece = lax.all_gather(folded, "fld", axis=3, tiled=True)
    parts_count = folded_piece.shape[2]
    width = folded_piece.shape[3]
    merged = folded_piece.reshape(slot_dev, 2, parts_count * width, folded_piece.shape[4])
    coeffs = jnp.einsum("sprj,spcj->srpc", legendre, merged, preferred_element_type=jnp.float32)
    coeffs = coeffs.reshape(slot_dev, row_dev, 2, parts_count, width)
    coeffs = coeffs * valid_mask[:, :, :, None, None]
    return coeffs.reshape(slot_dev, row_dev, -1)


LANES = 128
HALF = 64
MESH = pl.DeviceIdType.MESH
ARRIVALS = (
    (1, 1, 0), (1, 2, 0), (0, 0, 0), (0, 0, 1), (0, 1, 0), (1, 3, 0),
    (1, 4, 0), (1, 1, 1), (0, 2, 0), (1, 2, 1), (0, 3, 0), (1, 5, 0),
    (0, 1, 1), (1, 6, 0), (0, 2, 1), (1, 3, 1), (0, 4, 0), (1, 4, 1),
    (0, 5, 0), (0, 3, 1), (0, 6, 0), (1, 7, 0), (1, 6, 1), (1, 5, 1),
    (0, 4, 1), (0, 7, 0), (0, 6, 1), (1, 7, 1), (0, 5, 1), (0, 7, 1),
)
STRAIGHT = ()

def sin_cos_of_phase(phase, period):
    turns = jnp.floor(phase * (1.0 / period))
    rest = phase - turns * period
    rest = jnp.where(rest < 0, rest + period, rest)
    rest = jnp.where(rest >= period, rest - period, rest)
    eighth = period / 8
    q0 = rest < eighth
    q1 = rest < 3 * eighth
    q2 = rest < 5 * eighth
    q3 = rest < 7 * eighth
    centre = jnp.where(
        q0, 0.0, jnp.where(q1, 2 * eighth, jnp.where(q2, 4 * eighth, jnp.where(q3, 6 * eighth, period)))
    )
    x = (rest - centre) * (TWO_PI / period)
    y = x * x
    s = x * (1.0 + y * (-1 / 6 + y * (1 / 120 + y * (-1 / 5040 + y * (1 / 362880)))))
    c = 1.0 + y * (-1 / 2 + y * (1 / 24 + y * (-1 / 720 + y * (1 / 40320 - y * (1 / 3628800)))))
    even = q0 | (q2 & ~q1) | ~q3
    minus_sin = (q3 & ~q1)
    minus_cos = (q2 & ~q0)
    sine = jnp.where(even, s, c)
    sine = jnp.where(minus_sin, -sine, sine)
    cosine = jnp.where(even, c, s)
    cosine = jnp.where(minus_cos, -cosine, cosine)
    return sine, cosine


def transform_kernel(
    lat_count, wave_hbm, wave_row_hbm, field_ref, legendre_ref, out_ref,
    grid, twiddle, coarse, table, send, recv, folded, partial, spun, wave_smem, wave_row,
    field_sem, wave_sem, table_sem, sent, came,
):
    lat = lax.axis_index("lat")
    fld = lax.axis_index("fld")
    partner = fld + 1 - 2 * (fld % 2)
    core = fld % 2
    hub = fld + 1 - core
    hub_y = (hub + 2) % 4
    side = fld // 2
    first_chip = (lat == 0) & (side == 0)
    across = (lat == 0) & (side == 1)
    far = (lat >= lat_count // 2) & (fld == 2)

    _, lat_dev, lon_total = field_ref.shape
    main = lat_dev // LANES
    tiles = 2 * main + 1
    slot_dev, _, row_dev, _ = legendre_ref.shape
    slot_total = wave_row_hbm.shape[1]
    half_lats = lat_count // 2
    chunk_tiles = ((0, 1), (1, main + 1), (main + 1, tiles))
    chunk_count = len(chunk_tiles)

    def band_of(index):
        south = index // half_lats
        return south, index + south * (lat_count - 1 - 2 * index)

    def place_of(index):
        south, band = band_of(index)
        return 2 * band + south

    south, band = band_of(lat)
    place = place_of(lat)
    odd = band % 2
    mixed = (south + odd) % 2

    def chunk_of(t):
        return [low <= t < high for low, high in chunk_tiles].index(True)

    def load(f, row, count, dst):
        pltpu.make_async_copy(
            field_ref.at[f, pl.ds(pl.multiple_of(row, HALF), count)],
            grid.at[pl.ds(pl.multiple_of(dst, HALF), count)],
            field_sem.at[chunk_of(load_tile[0])],
        ).start(priority=1)

    load_tile = [0]

    def load_main(f, t, dst_tile):
        load_tile[0] = dst_tile
        north_row = LANES * t + HALF * odd
        south_row = lat_dev - LANES - LANES * t - HALF * odd
        load(f, north_row + south * (south_row - north_row), LANES, LANES * dst_tile)

    wave_copies = [
        pltpu.make_async_copy(wave_row_hbm, wave_row, wave_sem.at[0]),
        pltpu.make_async_copy(wave_hbm, wave_smem, wave_sem.at[1]),
    ]
    for copy in wave_copies:
        copy.start()
    for t in range(main):
        load_main(0, t, t)
    load_tile[0] = main
    tail_row = (lat_dev - HALF) * (1 - mixed)
    load(0, tail_row, HALF, LANES * main + HALF * mixed)
    load(1, tail_row, HALF, LANES * main + HALF * (1 - mixed))
    for t in range(main):
        load_main(1, t, main + 1 + t)

    barrier = pltpu.get_barrier_semaphore()

    @pl.when(core == 1)
    def _():
        for d in range(1, lat_count):
            for c in range(2):
                pl.semaphore_signal(
                    barrier, inc=1, device_id=((lat + d) % lat_count, hub - c), device_id_type=MESH
                )
        pl.semaphore_signal(barrier, inc=1, device_id=(lat, hub_y), device_id_type=MESH)

    @pl.when(core == 0)
    def _():
        pl.semaphore_signal(barrier, inc=1, device_id=(lat, hub_y), device_id_type=MESH)

    pl.semaphore_signal(barrier, inc=1, device_id=(lat, partner), device_id_type=MESH)

    @pl.when(first_chip & (core == 1))
    def _():
        for other in range(half_lats, lat_count):
            pl.semaphore_signal(barrier, inc=1, device_id=(other, 2), device_id_type=MESH)

    wave_copies[0].wait()
    waves = wave_row[...].astype(jnp.float32)
    waves = jnp.concatenate([waves, waves], axis=1)
    width = 2 * slot_total
    coarse_count = lon_total // LANES
    k_fine = lax.broadcasted_iota(jnp.int32, (LANES, width), 0).astype(jnp.float32)
    is_sine = lax.broadcasted_iota(jnp.int32, (LANES, width), 1) >= slot_total
    quarter = jnp.where(is_sine, lon_total / 4, 0.0)
    fine_sin, fine_cos = sin_cos_of_phase(waves * k_fine + quarter, lon_total)
    coarse_rows = coarse.shape[1]
    k_coarse = lax.broadcasted_iota(jnp.int32, (coarse_rows, width), 0).astype(jnp.float32) * LANES
    coarse_sin, coarse_cos = sin_cos_of_phase(waves * k_coarse, lon_total)
    coarse[0] = coarse_sin
    coarse[1] = coarse_cos
    for a in range(coarse_count):
        block = coarse[1, pl.ds(a, 1), :] * fine_cos - coarse[0, pl.ds(a, 1), :] * fine_sin
        twiddle[pl.ds(a * LANES, LANES), :] = block.astype(jnp.bfloat16)

    row = lax.broadcasted_iota(jnp.int32, (LANES, LANES), 0)
    column = lax.broadcasted_iota(jnp.int32, (LANES, LANES), 1)
    turned = row + south * (LANES - 1 - 2 * row)
    order = (turned == column).astype(jnp.float32).astype(jnp.bfloat16)

    def flipped(d):
        index, bit = lat, 1
        while bit < lat_count:
            if d & bit:
                index = index + bit * (1 - 2 * ((lat // bit) % 2))
            bit *= 2
        return index

    def columns(q):
        low, high = chunk_tiles[q]
        return pl.ds(low * LANES, (high - low) * LANES)

    def remote(src, dst, sent_at, recv_at, device):
        return pltpu.make_async_remote_copy(
            src_ref=src, dst_ref=dst, send_sem=sent.at[sent_at], recv_sem=recv_at,
            device_id=device, device_id_type=MESH,
        )

    middle = (lat // 2 + lat // 4) % 2
    came_from = 4 * lat_count - 2

    def peer(e):
        index = flipped(e)
        if e < half_lats:
            return index, e
        turned = middle * (1 - 2 * ((index // 2) % 2))
        return index + 2 * turned, e + 2 * middle * (1 - 2 * ((e // 2) % 2))

    def lat_sem(c, d, q):
        return came.at[(c * (lat_count - 1) + d) * 2 + (q == chunk_count - 1)]

    def y_sem(c, e, part):
        if isinstance(e, int) and e < half_lats:
            split = 0
        else:
            split = e // 2 - half_lats // 2 + 1 + 2 * part
        return came.at[came_from + c * 5 + split]

    def even_sem(source_place, part, group):
        if part == 0:
            return came.at[group]
        return came.at[4 * (1 - source_place // half_lats) + group]

    def part_columns(part):
        low = chunk_tiles[-1][0] if part else 0
        high = tiles if part else chunk_tiles[-1][0]
        return pl.ds(low * LANES, (high - low) * LANES)

    def straight_from_source(c, e, part):
        return c == 0 and e >= half_lats and part == 1

    def unless(skipped, chip, action):
        if skipped:
            pl.when(jnp.logical_not(chip))(action)
        else:
            action()

    def pass_on(src, group, source_place, c, e, where, part=0):
        there = recv.at[group, source_place, :, where]

        def cross():
            remote(src, there, 1, y_sem(c, e, part * (e >= half_lats)), (lat, hub_y)).start()
            if (c, e, part) in STRAIGHT:
                remote(
                    src, there, 1, even_sem(source_place, part, group), (lat, hub_y - 1)
                ).start()

        unless(straight_from_source(c, e, part), across, cross)
        remote(src, there, 2, even_sem(source_place, part, group), (lat, partner)).start()

    def send_chunk(q):
        for e in range(lat_count - 1, 0, -1):
            owner, d = peer(e)
            remote(
                send.at[owner, :, columns(q)], recv.at[fld, place, :, columns(q)],
                0, lat_sem(core, d, q), (owner, hub),
            ).start()

        if q == chunk_count - 1:
            @pl.when(far)
            def _():
                block = recv.at[fld, place, :, columns(q)]
                remote(send.at[0, :, columns(q)], block, 0, y_sem(0, lat, 1), (0, 1)).start()

        @pl.when(core == 1)
        def _():
            pass_on(send.at[lat, :, columns(q)], fld, place, 1, 0, columns(q), int(q == chunk_count - 1))
            recv[fld, place, :, columns(q)] = send[lat, :, columns(q)]

        @pl.when(core == 0)
        def _():
            remote(
                send.at[lat, :, columns(q)], recv.at[fld, place, :, columns(q)],
                2, lat_sem(0, 0, q), (lat, partner),
            ).start()

    patience = jnp.maximum(chunk_count - 1 - (lat // 2 + lat % 2), 0)
    greeted = lat_count + 2 * core + far.astype(jnp.int32)

    def release(q):
        @pl.when(patience == q)
        def _():
            pl.semaphore_wait(barrier, greeted)
            for k in range(q + 1):
                send_chunk(k)

        if q > 0:
            @pl.when(patience < q)
            def _():
                send_chunk(q)

    for q in range(chunk_count):
        low, high = chunk_tiles[q]
        rows = pl.ds(low * LANES, (high - low) * LANES)
        pltpu.make_async_copy(grid.at[rows], grid.at[rows], field_sem.at[q]).wait()
        spectra = jnp.dot(grid[rows, :], twiddle[...], preferred_element_type=jnp.float32)
        spectra = (spectra * (1.0 / lon_total)).astype(jnp.bfloat16)
        for t in range(low, high):
            part = spectra[(t - low) * LANES:(t - low + 1) * LANES, :]
            part = jnp.dot(order, part, preferred_element_type=jnp.float32)
            part = part.T
            for owner in range(lat_count):
                s0 = owner * slot_dev
                send[owner, :, pl.ds(t * LANES, LANES)] = jnp.concatenate(
                    [part[s0:s0 + slot_dev], part[slot_total + s0:slot_total + s0 + slot_dev]], axis=0
                ).astype(jnp.bfloat16)
        release(q)

    cut = main * LANES
    pair_lats = 2 * lat_dev
    spans = (
        (cut, 0, LANES),
        (pair_lats, LANES, pair_lats),
        (0, pair_lats + LANES, cut),
        (cut + LANES, pair_lats + LANES + cut, cut),
    )
    for source, target, count in spans:
        pltpu.make_async_copy(
            legendre_ref.at[:, :, :, pl.ds(source, count)],
            table.at[:, :, :, pl.ds(target, count)], table_sem,
        ).start()

    def relay(c, e, part):
        source, d = peer(e)
        group = hub - 1 + c
        source_place = place_of(source)
        here = recv.at[group, source_place, :, part_columns(part)]
        remote(here, here, 0, lat_sem(c, d, (chunk_count - 1) * part), (lat, partner)).wait_recv()
        pass_on(here, group, source_place, c, e, part_columns(part), part)

    def hand_over(c, pair, part=None):
        group = hub_y - 1 + c
        where = pl.ds(0, tiles * LANES) if part is None else part_columns(part)
        members = range(half_lats) if pair == 0 else (2 * pair, 2 * pair + 1)
        both = recv.at[group, pl.ds(0, len(members)), :, where]
        remote(both, both, 1, y_sem(c, 2 * pair, part or 0), (lat, hub_y)).wait_recv()
        for e in members:
            source_place = place_of(peer(e)[0])
            for k in (0, 1) if part is None else (part,):
                if (c, e, k) in STRAIGHT:
                    continue
                there = recv.at[group, source_place, :, part_columns(k)]
                hand = remote(there, there, 2, even_sem(source_place, k, group), (lat, partner))
                hand.start()

    def gather(*parts):
        for c, pair, part in parts:
            hand_over(c, pair, part)

    @pl.when(core == 1)
    def _():
        for c, e, part in ARRIVALS:
            relay(c, e, part)
        gather(
            (1, 2, 0), (0, 2, 0), (1, 0, None), (0, 0, None), (1, 3, 0), (1, 2, 1),
            (0, 3, 0), (0, 2, 1),
        )

    depth = 2 * slot_dev
    low_half = lax.broadcasted_iota(jnp.int32, (depth, LANES), 1) < HALF
    total_rows = 8 * depth
    trunc_total = 2 * row_dev * 4
    slot_of = lax.broadcasted_iota(jnp.int32, (row_dev, total_rows), 1) % slot_dev
    degree_row = 2 * (lax.broadcasted_iota(jnp.int32, (row_dev, total_rows), 0) + fld * row_dev)
    wave_copies[1].wait()
    wave_of = jnp.zeros((1, total_rows), jnp.int32)
    for s in range(slot_dev):
        wave_of = jnp.where(slot_of[:1] == s, wave_smem[lat * slot_dev + s], wave_of)
    pltpu.make_async_copy(table, table, table_sem).wait()
    widths = (pair_lats + LANES, 2 * cut)

    def fold(h, keep):
        for group in range(4):
            north = [recv[group, 2 * (2 * h + o), :, keep].astype(jnp.float32) for o in range(2)]
            mirror = [recv[group, 2 * (2 * h + o) + 1, :, keep].astype(jnp.float32) for o in range(2)]
            for p in range(2):
                yield group, p, [n + m if p == 0 else n - m for n, m in zip(north, mirror)]

    def put(group, p, f, start, value):
        rows = pl.ds((2 * group + f) * depth, depth)
        folded[p, rows, pl.ds(start, value.shape[1])] = value.astype(jnp.bfloat16)

    def put_middle(group, p, bands, start):
        mid_even, mid_odd = bands
        put(group, p, 0, start, jnp.where(low_half, mid_even, mid_odd))
        put(
            group, p, 1, start,
            pltpu.roll(jnp.where(low_half, mid_odd, mid_even), HALF, 1),
        )

    for phase in range(2):
        base = phase * widths[0]
        @pl.when(core == 0)
        def _():
            for group in range(4):
                if phase == 0:
                    block = recv.at[group, :, :, pl.ds(0, (tiles + main + 1) // 2 * LANES)]
                else:
                    block = recv.at[group, pl.ds(0, half_lats), :, part_columns(1)]
                remote(block, block, 2, came.at[4 * phase + group], (lat, partner)).wait_recv()

        if phase == 0:
            for group, p, bands in fold(0, pl.ds(cut, LANES)):
                put_middle(group, p, bands, 0)
            for group, p, (even_band, odd_band) in fold(1, slice(None)):
                for f in range(2):
                    start = f * (cut + LANES)
                    put(group, p, f, LANES, even_band[:, start:start + cut])
                    put(group, p, f, LANES + cut + LANES, odd_band[:, start:start + cut])
                put_middle(
                    group, p, [band[:, cut:cut + LANES] for band in (even_band, odd_band)], LANES + cut
                )
        else:
            for f in range(2):
                for group, p, bands in fold(0, pl.ds(f * (cut + LANES), cut)):
                    for o in range(2):
                        put(group, p, f, base + o * cut, bands[o])
        for p in range(2):
            if phase == 0 and p == 1:
                @pl.when(core == 1)
                def _():
                    gather((1, 3, 1), (0, 3, 1))

            kept = jnp.zeros((row_dev, total_rows), jnp.float32)
            for first in range(0, slot_dev, 2):
                sums = lax.dot_general(
                    table[first:first + 2, p, :, pl.ds(base, widths[phase])].reshape(
                        2 * row_dev, widths[phase]
                    ),
                    folded[p, :, pl.ds(base, widths[phase])],
                    (((1,), (1,)), ((), ())), preferred_element_type=jnp.float32,
                )
                for s in range(2):
                    kept = jnp.where(slot_of == first + s, sums[s * row_dev:(s + 1) * row_dev], kept)
            if phase == 0:
                partial[p] = kept
                continue
            kept = jnp.where(degree_row + (wave_of + p) <= trunc_total - 1, kept + partial[p], 0.0)
            padded = jnp.concatenate(
                [kept, jnp.zeros((spun.shape[1] * LANES - row_dev, total_rows), jnp.float32)], axis=0
            )
            for t in range(spun.shape[1]):
                spun[p, t] = padded[t * LANES:(t + 1) * LANES].T
    for s in range(slot_dev):
        for p in range(2):
            for c in range(2):
                for t in range(spun.shape[1]):
                    kept_rows = min(LANES, row_dev - t * LANES)
                    out_ref[s, pl.ds(p * 16 + c * 8, 8), pl.ds(t * LANES, kept_rows)] = spun[
                        p, t, pl.ds(c * slot_dev + s, 8, stride=depth), :
                    ][:, :kept_rows]
    def drain(kind, block):
        remote(block, block, kind, table_sem, (lat, partner)).wait_send()

    drain(0, recv.at[fld, pl.ds(0, lat_count - 1)])

    @pl.when(far)
    def _():
        drain(0, recv.at[0, 0, :, part_columns(1)])

    @pl.when(core == 1)
    def _():
        def drain_parts(kind, chip, events):
            for part in range(2):
                where = part_columns(part)
                skipped = [v for v in events if v[2] == part and straight_from_source(*v)]
                others = skipped if chip is not None else []
                always = [v for v in events if v[2] == part and v not in others]
                for start in range(0, len(always), lat_count):
                    count = min(lat_count, len(always) - start)
                    drain(kind, recv.at[0, pl.ds(0, count), :, where])
                if others:
                    @pl.when(jnp.logical_not(chip))
                    def _():
                        drain(kind, recv.at[0, pl.ds(0, len(others)), :, where])

        pieces = [(c, e, part) for c in range(2) for e in range(lat_count) for part in range(2)]
        drain_parts(1, across, pieces + list(STRAIGHT))
        drain(2, recv.at[pl.ds(0, 2)])
        drain_parts(2, None, [v for v in pieces if v not in STRAIGHT])

    @pl.when(core == 0)
    def _():
        drain(2, recv.at[0, 0])


def shards_by_kernel(field_grid, wave_table, legendre):
    f_dev, lat_dev, lon_total = field_grid.shape
    slot_dev, _, row_dev, north_total = legendre.shape
    slot_total = wave_table.shape[0]
    lat_count = lax.axis_size("lat")
    rows = f_dev * lat_dev
    bf16, f32 = jnp.bfloat16, jnp.float32
    dma = pltpu.SemaphoreType.DMA
    padded_rows = -(-row_dev // LANES) * LANES
    coarse_rows = -(-(lon_total // LANES) // 8) * 8
    vmem, smem = pltpu.VMEM, pltpu.SMEM
    out = pl.pallas_call(
        functools.partial(transform_kernel, lat_count),
        out_shape=pltpu.VMEM((slot_dev, 32, row_dev), f32),
        in_specs=[pl.BlockSpec(memory_space=pl.ANY)] * 4,
        out_specs=pl.BlockSpec(memory_space=vmem),
        scratch_shapes=[
            vmem((rows, lon_total), bf16),
            vmem((lon_total, 2 * slot_total), bf16),
            vmem((2, coarse_rows, 2 * slot_total), f32),
            vmem(legendre.shape, bf16),
            vmem((lat_count, 2 * slot_dev, rows), bf16),
            vmem((4, lat_count, 2 * slot_dev, rows), bf16),
            vmem((2, 16 * slot_dev, north_total), bf16),
            vmem((2, row_dev, 16 * slot_dev), f32),
            vmem((2, padded_rows // LANES, 16 * slot_dev, LANES), f32),
            smem((slot_total,), jnp.int32),
            vmem((1, slot_total), jnp.int32),
            dma((3,)),
            dma((2,)),
            dma(()),
            dma((3,)),
            dma((4 * lat_count + 8,)),
        ],
        compiler_params=pltpu.CompilerParams(
            collective_id=0, has_side_effects=True
        ),
    )(wave_table, wave_table.reshape(1, slot_total), field_grid, legendre)
    return jnp.transpose(out, (0, 2, 1))


def shards(field_grid, wave_table, legendre):
    f_dev, lat_dev, lon_total = field_grid.shape
    slot_dev, _, row_dev, _ = legendre.shape
    slot_total = wave_table.shape[0]
    fits = (
        f_dev == 2
        and slot_dev == 8
        and 2 * slot_total == LANES
        and lat_dev % LANES == HALF
        and lat_dev // LANES % 2 == 0
        and lat_dev > LANES
        and lax.axis_size("fld") == 4
        and lax.axis_size("lat") == 8
        and lon_total % LANES == 0
        and row_dev % 8 == 0
        and 2 * row_dev * 4 * lon_total < 2**24
    )
    if fits:
        return shards_by_kernel(field_grid, wave_table, legendre)
    return shards_by_collectives(field_grid, wave_table, legendre)


def solution(mesh):
    placed = (P("fld", "lat", None), P(), P("lat", None, "fld", None))
    return jax.shard_map(
        shards, mesh=mesh, in_specs=placed, out_specs=P("lat", "fld", None), check_vma=False
    )
```
